32 devices in a mesh: circ: 4 (over y, x), span: 8 (over z, core).
Axes of the slice: x: 2, y: 2, z: 4, core: 2. Of those that a mesh axis runs over, the one named last changes fastest.
Arguments:
- elem_rows: bfloat16 [80, 24576], P(None, ('circ', 'span')), may hold values from -6 to 6
- coupling: bfloat16 [24, 80, 80, 1024], P('circ', None, None, 'span')
- inverses: bfloat16 [24, 80, 80, 1024], P('circ', None, None, 'span'), may hold values from -0.625 to 0.625
- send_rows: int32 [32, 32, 48], P(('circ', 'span')), may hold values from 0 to 767, as said below
- recv_cells: int32 [32, 32, 48], P(('circ', 'span')), may hold values from 0 to 767, as said below
- slot_counts: int32 [32, 32], P(('circ', 'span')), may hold values from 0 to 48, as said below
Outputs:
- corrections: float32 [80, 24576], P(None, ('circ', 'span'))
The draws below stay inside these ranges and needn't reach their ends.
Inputs may be any that keep to these rules, and one draw needn't show every extreme that they name: `send_rows`: each source's filled slots name each of its 768 rows exactly once, each owner's filled slots name each of its 768 cells exactly once; unfilled slots hold 0. `recv_cells`: as send_rows, for the owners' cells. `slot_counts`: every owner's counts sum to 768, and so do every source's; some pair fills all 48 slots.
All inputs are finite; a program needn't handle non-finite values.
Results may differ from the reference program's by a relative error of at most 0.0003.
Values may be sent and summed in bfloat16 or wider, within the bound.
A program may use at most 128 MiB of HBM per device.

```python
import jax
import jax.numpy as jnp
from jax import lax

W = 80
CPD = 6
NLINE = 128
CELLS = 768
CAP = 48
CIRCUIT_ZONES = 24
OVERALL_STRANDS = 1024
ROWS = 24576
N_CIRC = 4
N_SPAN = 8
DEVICES = 32


def routing_tables(key):
    key_order, key_mags, key_label, key_rows, key_cells = jax.random.split(jax.random.fold_in(key, 7), 5)
    base = CELLS // DEVICES
    half = DEVICES // 2
    order = jax.random.permutation(key_order, DEVICES)
    magnitudes = jax.random.randint(key_mags, (half,), 0, base + 1).astype(jnp.int32)
    magnitudes = magnitudes.at[0].set(base)
    offsets = jnp.zeros((DEVICES,), jnp.int32).at[order[:half]].set(magnitudes).at[order[half:]].set(-magnitudes)
    relabel = jax.random.permutation(key_label, DEVICES)
    source_index = jnp.arange(DEVICES, dtype=jnp.int32)[:, None]
    target_index = jnp.arange(DEVICES, dtype=jnp.int32)[None, :]
    counts = (base + offsets[(relabel[target_index] - source_index) % DEVICES]).astype(jnp.int32)
    slot_index = jnp.arange(CAP, dtype=jnp.int32)[None, None, :]
    row_perms = jax.vmap(lambda sub: jax.random.permutation(sub, CELLS))(jax.random.split(key_rows, DEVICES)).astype(jnp.int32)
    starts = jnp.cumsum(counts, axis=1) - counts
    places = jnp.clip(starts[:, :, None] + slot_index, 0, CELLS - 1)
    picked = jax.vmap(lambda table, where_at: table[where_at])(row_perms, places)
    send_table = jnp.where(slot_index < counts[:, :, None], picked, 0).astype(jnp.int32)
    owner_counts = jnp.transpose(counts)
    cell_perms = jax.vmap(lambda sub: jax.random.permutation(sub, CELLS))(jax.random.split(key_cells, DEVICES)).astype(jnp.int32)
    owner_starts = jnp.cumsum(owner_counts, axis=1) - owner_counts
    owner_places = jnp.clip(owner_starts[:, :, None] + slot_index, 0, CELLS - 1)
    owner_picked = jax.vmap(lambda table, where_at: table[where_at])(cell_perms, owner_places)
    recv_table = jnp.where(slot_index < owner_counts[:, :, None], owner_picked, 0).astype(jnp.int32)
    return (send_table, recv_table, owner_counts)


def draw_send_rows(key, part):
    return routing_tables(key)[0]


def draw_recv_cells(key, part):
    return routing_tables(key)[1]


def draw_slot_counts(key, part):
    return routing_tables(key)[2]


def draw_coupling(key, part):
    random_coefficient_stream, random_drawn_attenuation, random_exponent_choice, random_steep_attenuation, random_jump_choice = jax.random.split(jax.random.fold_in(key, 11), 5)
    entries = jax.random.normal(random_coefficient_stream, (CIRCUIT_ZONES, W, W, OVERALL_STRANDS), jnp.float32) / jnp.sqrt(W * 1.0)
    slow = jax.random.bernoulli(random_drawn_attenuation, 0.5, (OVERALL_STRANDS,))
    gentle = jax.random.uniform(random_exponent_choice, (OVERALL_STRANDS,), jnp.float32, 0.0, 0.5)
    strong = jax.random.uniform(random_steep_attenuation, (OVERALL_STRANDS,), jnp.float32, CIRCUIT_ZONES / 12.0, CIRCUIT_ZONES / 6.0)
    decay = jnp.where(slow, gentle, strong)
    attenuation_exponent = jnp.exp(-decay / CIRCUIT_ZONES)
    jump_places_chosen = jax.random.randint(random_jump_choice, (2, OVERALL_STRANDS), 0, CIRCUIT_ZONES)
    zone_ordinal_labels = jnp.arange(CIRCUIT_ZONES, dtype=jnp.int32)[:, None]
    jump_families = jnp.where(zone_ordinal_labels == jump_places_chosen[0][None, :], 0.75, 1.0) * jnp.where(zone_ordinal_labels == jump_places_chosen[1][None, :], 0.75, 1.0)
    magnitude_ratios = attenuation_exponent[None, :] * jump_families
    return (entries * magnitude_ratios[:, None, None, :]).astype(jnp.bfloat16)


def block_levels(key, shape, cuts, smallest, top_value):
    level = 1.0
    for dim, parts in cuts:
        heights = jax.random.uniform(jax.random.fold_in(jax.random.fold_in(key, 6), dim), (parts,), jnp.float32, smallest / len(cuts), top_value / len(cuts))
        level = level * jnp.repeat(jnp.exp(heights), shape[dim] // parts).reshape((-1,) + (1,) * (len(shape) - 1 - dim))
    return level


def scatter_about(stream_key, dims, width, most, cuts=(), kind=jnp.bfloat16):
    gain = block_levels(stream_key, dims, cuts, -0.22, 0.18) if cuts else 1.0
    values = jax.random.normal(stream_key, dims, jnp.float32) * width * gain
    return jnp.minimum(jnp.maximum(values, -most), most).astype(kind)


def setup_inputs(seed: int = 0) -> dict:
    arg_keys = jax.random.split(jax.random.key(seed), 7)
    return {
        "elem_rows": scatter_about(arg_keys[0], (W, ROWS), 1.0, 6.0, ((1, 32),)),
        "coupling": draw_coupling(jax.random.fold_in(arg_keys[6], 71), 0),
        "inverses": scatter_about(arg_keys[2], (CIRCUIT_ZONES, W, W, OVERALL_STRANDS), W ** -0.5, 0.625, ((0, 4), (3, 8))),
        "send_rows": draw_send_rows(jax.random.fold_in(arg_keys[6], 71), 0),
        "recv_cells": draw_recv_cells(jax.random.fold_in(arg_keys[6], 71), 0),
        "slot_counts": draw_slot_counts(jax.random.fold_in(arg_keys[6], 71), 0),
    }


def line_turn(coupling, inverses, line_res, incoming):
    def advance(current, position):
        forcing = jnp.einsum('ijn,jn->in', inverses[position].astype(jnp.float32), line_res[position], precision=lax.Precision.HIGHEST)
        moved = jnp.einsum('ijn,jn->in', coupling[position].astype(jnp.float32), current, precision=lax.Precision.HIGHEST)
        following = forcing + moved
        return following, following
    return lax.scan(advance, incoming, jnp.arange(CIRCUIT_ZONES, dtype=jnp.int32))


def reference(elem_rows, coupling, inverses, send_rows, recv_cells, slot_counts):
    slot_index = jnp.arange(CAP, dtype=jnp.int32)
    source_index = jnp.arange(DEVICES, dtype=jnp.int32)
    filled = slot_index[None, None, :] < jnp.transpose(slot_counts)[:, :, None]
    source_cols = (source_index[:, None, None] * CELLS + send_rows).astype(jnp.int32)
    owner_cells = jnp.transpose(recv_cells, (1, 0, 2))
    target_cols = (source_index[None, :, None] * CELLS + owner_cells).astype(jnp.int32)
    dropped = jnp.where(filled, target_cols, ROWS).astype(jnp.int32)
    line_rows = jnp.zeros((W, ROWS), jnp.bfloat16).at[:, dropped.reshape(-1)].set(elem_rows[:, source_cols.reshape(-1)], mode="drop")
    shaped = line_rows.reshape(W, N_CIRC, N_SPAN, CPD, NLINE)
    line_res = jnp.transpose(shaped, (1, 3, 0, 2, 4)).reshape(CIRCUIT_ZONES, W, OVERALL_STRANDS).astype(jnp.float32)
    nothing = jnp.zeros((W, OVERALL_STRANDS), jnp.float32)
    loop_last, unused = line_turn(coupling, inverses, line_res, nothing)
    unused_end, solved = line_turn(coupling, inverses, line_res, loop_last)
    solved = jnp.transpose(solved.reshape(N_CIRC, CPD, W, N_SPAN, NLINE), (2, 0, 3, 1, 4)).reshape(W, ROWS)
    values = solved[:, jnp.clip(target_cols, 0, ROWS - 1).reshape(-1)]
    back_cols = jnp.where(filled, source_cols, ROWS).astype(jnp.int32)
    return jnp.zeros((W, ROWS), jnp.float32).at[:, back_cols.reshape(-1)].set(values, mode="drop")
```

```python
import functools

import jax
import jax.numpy as jnp
from jax import lax
from jax.experimental import pallas as pl
from jax.experimental.pallas import tpu as pltpu
from jax.sharding import PartitionSpec as P

MESH = pl.DeviceIdType.MESH
GROUPS = 4


def merge(low, high, half, mask):
    if 2 * half == low.shape[0]:
        return jnp.where(mask, low, high) + pltpu.roll(jnp.where(mask, high, low), half, axis=0)
    back = low.shape[0] - half
    return jnp.where(mask, low + pltpu.roll(low, back, axis=0), high + pltpu.roll(high, half, axis=0))


def fold(parts):
    row = lax.broadcasted_iota(jnp.int32, parts[0].shape, 0)
    half = len(parts) // 2
    while half:
        mask = (row & half) == 0
        parts = [merge(parts[i], parts[i + half], half, mask) for i in range(half)]
        half //= 2
    return parts[0]


def block_rows(mat_ref, position, base, vector):
    width = vector.shape[0]
    parts = []
    for i in range(8):
        total = None
        for start in range(0, width, 16):
            piece = mat_ref[position, base + i, start : start + 16, :]
            term = piece.astype(jnp.float32) * vector[start : start + 16]
            total = term if total is None else total + term
        parts.append(total[:8] + total[8:])
    return fold(parts)


def relay_kernel(
    n_circ, rows_ref, inv_hbm, coup_hbm, out_ref, inv, coup, forcing, state, inbox, outbox, inv_sem, coup_sem, send_sem, recv_sem
):
    me = lax.axis_index("circ")
    right, left = lax.rem(me + 1, n_circ), lax.rem(me + n_circ - 1, n_circ)
    segment, width = coup.shape[0], coup.shape[1]
    blocks = width // 8

    loads = [pltpu.make_async_copy(inv_hbm.at[k], inv.at[k], inv_sem.at[k]) for k in range(segment)]
    loads += [pltpu.make_async_copy(coup_hbm.at[k], coup.at[k], coup_sem.at[k]) for k in range(segment)]
    for load in loads:
        load.start()

    barrier = pltpu.get_barrier_semaphore()
    for neighbour in (left, right):
        pl.semaphore_signal(barrier, inc=1, device_id={"circ": neighbour}, device_id_type=MESH)
    pl.semaphore_wait(barrier, 2)

    for k in range(segment):
        loads[k].wait()
        vector = rows_ref[k].astype(jnp.float32)

        def force(b, _, k=k, vector=vector):
            base = pl.multiple_of(b * 8, 8)
            forcing[k, pl.ds(base, 8), :] = block_rows(inv, k, base, vector)
            return 0

        lax.fori_loop(0, blocks, force, 0)
    for k in range(segment):
        loads[segment + k].wait()

    def hop(turn, slot):
        return pltpu.make_async_remote_copy(
            src_ref=outbox.at[turn],
            dst_ref=inbox.at[slot],
            send_sem=send_sem.at[turn],
            recv_sem=recv_sem.at[slot],
            device_id={"circ": right},
            device_id_type=MESH,
        )

    def sweep(target):
        def step(k, _):
            vector = state[...]

            def advance(b, _):
                base = pl.multiple_of(b * 8, 8)
                value = forcing[k, pl.ds(base, 8), :] + block_rows(coup, k, base, vector)
                state[pl.ds(base, 8), :] = value
                if target is not None:
                    target[k, pl.ds(base, 8), :] = value
                return 0

            lax.fori_loop(0, blocks, advance, 0)
            return 0

        lax.fori_loop(0, segment, step, 0)

    @pl.when(me == 0)
    def _():
        state[...] = jnp.zeros_like(state)

    @pl.when(me > 0)
    def _():
        hop(0, 0).wait_recv()
        state[...] = inbox[0]

    sweep(None)
    outbox[0] = state[...]
    slot = jnp.where(me == n_circ - 1, 1, 0)
    first = hop(0, slot)
    first.start()
    hop(0, 1).wait_recv()
    state[...] = inbox[1]
    sweep(out_ref)

    @pl.when(me < n_circ - 1)
    def _():
        outbox[1] = state[...]
        second = hop(1, 1)
        second.start()
        second.wait_send()

    first.wait_send()


def relay(rows, inverses, coupling):
    segment, width, _, lines = coupling.shape
    n_circ = lax.axis_size("circ")
    state = pltpu.VMEM((width, lines), jnp.float32)
    boxes = pltpu.VMEM((2, width, lines), jnp.float32)
    return pl.pallas_call(
        functools.partial(relay_kernel, n_circ),
        out_shape=jax.ShapeDtypeStruct((segment, width, lines), jnp.float32),
        in_specs=[
            pl.BlockSpec(memory_space=pltpu.VMEM),
            pl.BlockSpec(memory_space=pl.ANY),
            pl.BlockSpec(memory_space=pl.ANY),
        ],
        out_specs=pl.BlockSpec(memory_space=pltpu.VMEM),
        scratch_shapes=[
            pltpu.VMEM(inverses.shape, jnp.bfloat16),
            pltpu.VMEM(coupling.shape, jnp.bfloat16),
            pltpu.VMEM((segment, width, lines), jnp.float32),
            state,
            boxes,
            boxes,
            pltpu.SemaphoreType.DMA((segment,)),
            pltpu.SemaphoreType.DMA((segment,)),
            pltpu.SemaphoreType.DMA((2,)),
            pltpu.SemaphoreType.DMA((2,)),
        ],
        compiler_params=pltpu.CompilerParams(
            collective_id=0, has_side_effects=True, vmem_limit_bytes=48 * 1024 * 1024
        ),
        name="relay",
    )(rows, inverses, coupling)


def staged(elem_rows, coupling, inverses, send_rows, recv_cells, slot_counts):
    features, cell_count = elem_rows.shape
    peer_count, slot_count = (send_rows.shape[1], send_rows.shape[2])
    segment, line_count = (coupling.shape[0], coupling.shape[3])
    outgoing = jnp.take(elem_rows, send_rows[0].reshape(-1), axis=1).reshape(
        features, peer_count, slot_count
    )
    arrived = lax.all_to_all(outgoing, ("circ", "span"), split_axis=1, concat_axis=1, tiled=True)
    filled = jnp.arange(slot_count, dtype=jnp.int32)[None, :] < slot_counts[0][:, None]
    targets = jnp.where(filled, recv_cells[0], cell_count).reshape(-1)
    line_rows = (
        jnp.zeros((features, cell_count), jnp.bfloat16)
        .at[:, targets]
        .set(arrived.reshape(features, -1), mode="drop")
    )
    line_cells = jnp.transpose(line_rows.reshape(features, segment, line_count), (1, 0, 2))
    states = relay(line_cells, inverses, coupling)
    solved = jnp.transpose(states, (1, 0, 2)).reshape(features, cell_count)
    returning = jnp.take(solved, recv_cells[0].reshape(-1), axis=1).reshape(
        features, peer_count, slot_count
    )
    returning = jnp.where(filled[None, :, :], returning, 0.0)
    returned = lax.all_to_all(returning, ("circ", "span"), split_axis=1, concat_axis=1, tiled=True)
    return (
        jnp.zeros((features, cell_count), jnp.float32)
        .at[:, send_rows[0].reshape(-1)]
        .add(returned.reshape(features, -1))
    )


def code(values, lane, width, extra):
    size = jnp.abs(values)
    tiny = jnp.float32(1e-36)
    top_main = jnp.max(jnp.where(lane < width, size, tiny), axis=1, keepdims=True)
    top_extra = jnp.max(jnp.where(lane < width, tiny, size), axis=1, keepdims=True)
    power_main = jnp.ceil(jnp.log2(jnp.maximum(top_main, tiny)))
    power_extra = jnp.ceil(jnp.log2(jnp.maximum(top_extra, tiny)))
    root = jnp.exp2(-0.5 * jnp.where(lane < width, power_main, power_extra))
    whole = jnp.round(values * root * root * 32000.0)
    whole = jnp.where(lane == width + extra, power_main, whole)
    whole = jnp.where(lane == width + extra + 1, power_extra, whole)
    return whole.astype(jnp.int32).astype(jnp.int16)


def decode(coded, lane, width, extra):
    whole = coded.astype(jnp.int32).astype(jnp.float32)
    power_main = jnp.sum(jnp.where(lane == width + extra, whole, 0.0), axis=1, keepdims=True)
    power_extra = jnp.sum(jnp.where(lane == width + extra + 1, whole, 0.0), axis=1, keepdims=True)
    root = jnp.exp2(0.5 * jnp.where(lane < width, power_main, power_extra))
    return jnp.where(lane < width + extra, whole * (1.0 / 32000.0) * root * root, 0.0)


def split(values):
    high = values.astype(jnp.bfloat16)
    return high, (values - high.astype(jnp.float32)).astype(jnp.bfloat16)


def nt(a, b):
    return lax.dot_general(a, b, (((1,), (1,)), ((), ())), preferred_element_type=jnp.float32)


def nn(a, b):
    return jnp.dot(a, b, preferred_element_type=jnp.float32)


def spread(table):
    width, cells = table.shape
    half = width // 2
    head = jnp.zeros((width, cells), jnp.float32)
    tail = jnp.zeros((128 - width - half, cells), jnp.float32)
    return (
        jnp.concatenate([table, jnp.zeros((128 - width, cells), jnp.float32)], axis=0),
        jnp.concatenate([head, table[:half], tail], axis=0),
        jnp.concatenate([head, table[half:], tail], axis=0),
    )


def turn_lanes(values):
    count = len(values)
    lane = lax.broadcasted_iota(jnp.int32, values[0].shape, 1)
    size = values[0].shape[1]
    step = count // 2
    while step:
        wide = size // count * step
        upper = (lane & wide) != 0
        swapped = list(values)
        for i in range(count):
            if i & step == 0:
                low, high = values[i], values[i + step]
                swapped[i] = jnp.where(upper, pltpu.roll(high, wide, axis=1), low)
                swapped[i + step] = jnp.where(upper, high, pltpu.roll(low, size - wide, axis=1))
        values = swapped
        step //= 2
    return values


def fill_lanes(value, count):
    size = value.shape[1]
    lane = lax.broadcasted_iota(jnp.int32, value.shape, 1)
    values = [value]
    step = count // 2
    while step:
        wide = size // count * step
        upper = (lane & wide) != 0
        grown = []
        for held in values:
            moved = pltpu.roll(held, wide, axis=1)
            if 2 * wide != size:
                back = pltpu.roll(held, size - wide, axis=1)
            else:
                back = moved
            grown += [jnp.where(upper, moved, held), jnp.where(upper, held, back)]
        values = grown
        step //= 2
    return values


def halves(tile):
    low = lax.broadcasted_iota(jnp.int32, tile.shape, 0) < 4
    moved = pltpu.roll(tile, 4, axis=0)
    return jnp.where(low, tile, moved), jnp.where(low, moved, tile)


def joined(first, second):
    low = lax.broadcasted_iota(jnp.int32, first.shape, 0) < 4
    return jnp.where(low, first, second)


def row_plan(width, groups):
    full = width // 8 // groups
    spare = (width // 8 - full * groups) * 8 // groups
    return full, spare


def to_groups(tiles, groups):
    full, spare = row_plan(8 * len(tiles), groups)
    rows = [turn_lanes(tiles[b * groups : (b + 1) * groups]) for b in range(full)]
    if spare:
        pieces = [piece for tile in tiles[full * groups :] for piece in halves(tile)]
        rows.append(turn_lanes(pieces))
    return [[row[g] for row in rows] for g in range(groups)]


def from_groups(packed, width):
    groups = len(packed)
    full, spare = row_plan(width, groups)
    tiles = []
    for b in range(full):
        tiles += turn_lanes([packed[g][b] for g in range(groups)])
    if spare:
        pieces = turn_lanes([packed[g][full] for g in range(groups)])
        tiles += [joined(pieces[i], pieces[i + 1]) for i in range(0, groups, 2)]
    return tiles


def replicate(rows, width, groups):
    full, spare = row_plan(width, groups)
    tiles = []
    for b in range(full):
        tiles += fill_lanes(rows[b], groups)
    if spare:
        pieces = fill_lanes(rows[full], groups)
        tiles += [joined(pieces[i], pieces[i + 1]) for i in range(0, groups, 2)]
    return tiles


def advance(wide, group, position, tiles, add, width, groups):
    full, spare = row_plan(width, groups)
    rows = []
    for b in range(full + (spare > 0)):
        parts = []
        for i in range(8 if b < full else spare):
            total = None
            for t, tile in enumerate(tiles):
                term = wide[group, position, 8 * b + i, 8 * t : 8 * t + 8, :] * tile
                total = term if total is None else total + term
            parts.append(total)
        value = fold(parts)
        if b == full:
            value = value + pltpu.roll(value, 4, axis=0)
        rows.append(value + add[b])
    return rows


def fused_kernel(
    n_circ, n_span, groups, elem_ref, send_ref, recv_ref, count_ref, inv_hbm, coup_hbm, out_ref,
    inv, coup, wide, line_rows, forcing, parts_in, solved, inbox, outbox, pick_send, pick_recv, sent, arrived, back_sent, back_arrived,
    inv_sem, coup_sem, send_sem, recv_sem, go_send, go_recv, back_send, back_recv,
):
    circ, span = lax.axis_index("circ"), lax.axis_index("span")
    peers = n_circ * n_span
    me = circ * n_span + span
    right = lax.rem(circ + 1, n_circ)
    segment, width, lines = forcing.shape
    cells = segment * lines
    third = sent.shape[1] // 2
    half = width // 2
    blocks = width // 8

    coup_loads = [pltpu.make_async_copy(coup_hbm.at[k], coup.at[k], coup_sem.at[k]) for k in range(segment)]
    inv_loads = [pltpu.make_async_copy(inv_hbm.at[k], inv.at[k], inv_sem.at[k]) for k in range(segment)]
    for load in coup_loads + inv_loads:
        load.start()

    barrier = pltpu.get_barrier_semaphore()

    def greet(o, _):
        peer = lax.rem(me + o, peers)
        pl.semaphore_signal(
            barrier, inc=1, device_id={"circ": peer // n_span, "span": peer % n_span}, device_id_type=MESH
        )
        return 0

    lax.fori_loop(1, peers, greet, 0)

    def build(index_ref, pick, masked):
        lane = lax.broadcasted_iota(jnp.int32, (third, index_ref.shape[1]), 1)
        slot = lax.broadcasted_iota(jnp.int32, (third, index_ref.shape[1]), 0)
        number = lax.broadcasted_iota(jnp.int32, (third, cells), 1).astype(jnp.float32)
        owner = lax.broadcasted_iota(jnp.int32, count_ref.shape, 1)
        rank = lax.broadcasted_iota(jnp.int32, (third, 1), 0).astype(jnp.float32)

        def one(p, _):
            row = index_ref[pl.ds(p, 1), :].astype(jnp.float32)
            if masked:
                counts = count_ref[...].astype(jnp.float32)
                count = jnp.sum(jnp.where(owner == p, counts, 0.0), axis=1, keepdims=True)
            for t in range(3):
                column = jnp.sum(jnp.where(lane == slot + t * third, row, 0.0), axis=1, keepdims=True)
                if masked:
                    column = jnp.where(rank + float(t * third) < count, column, -1.0)
                hot = jnp.where(number == column, 1.0, 0.0).astype(jnp.bfloat16)
                pick[t, pl.ds(pl.multiple_of(p * third, third), third), :] = hot
            return 0

        lax.fori_loop(0, peers, one, 0)

    def exchange(outs, ins, outs_sem, ins_sem):
        def copy(peer, landing):
            return pltpu.make_async_remote_copy(
                src_ref=outs.at[peer],
                dst_ref=ins.at[landing],
                send_sem=outs_sem.at[peer],
                recv_sem=ins_sem.at[landing],
                device_id={"circ": peer // n_span, "span": peer % n_span},
                device_id_type=MESH,
            )

        def start(o, _):
            peer = o // n_span * n_span + lax.rem(span + o, n_span)

            @pl.when(peer != me)
            def _():
                copy(peer, me).start()

            return 0

        def land(o, _):
            peer = lax.rem(me + peers - o, peers)
            copy(peer, peer).wait_recv()
            return 0

        def drain(o, _):
            copy(lax.rem(me + o, peers), me).wait_send()
            return 0

        return (
            lambda: lax.fori_loop(0, peers, start, 0),
            lambda: lax.fori_loop(1, peers, land, 0),
            lambda: lax.fori_loop(1, peers, drain, 0),
        )

    build(send_ref, pick_send, False)
    whole, low, high = [w.astype(jnp.bfloat16) for w in spread(elem_ref[...].astype(jnp.float32))]
    first = nt(pick_send[0], whole) + nt(pick_send[2], low)
    second = nt(pick_send[1], whole) + nt(pick_send[2], high)
    sent[:, :third, :] = first.astype(jnp.bfloat16).reshape(peers, third, 128)
    sent[:, third:, :] = second.astype(jnp.bfloat16).reshape(peers, third, 128)

    pl.semaphore_wait(barrier, peers - 1)
    start, land, drain_go = exchange(sent, arrived, go_send, go_recv)
    start()
    arrived[me] = sent[me]
    build(recv_ref, pick_recv, True)
    full, spare = row_plan(width, groups)
    for k in range(segment):
        coup_loads[k].wait()

        def widen(row, _, k=k):
            first = row // 8 * (8 * groups) + lax.rem(row, 8)
            for start in range(0, width, 16):
                pieces = [coup[k, first + 8 * a, start : start + 16, :].astype(jnp.float32) for a in range(groups)]
                for g, piece in enumerate(turn_lanes(pieces)):
                    wide[g, k, row, start : start + 16, :] = piece
            return 0

        lax.fori_loop(0, 8 * full, widen, 0)

        def widen_spare(row, _, k=k):
            first = 8 * full * groups + row
            for start in range(0, width, 16):
                pieces = [coup[k, first + spare * a, start : start + 16, :].astype(jnp.float32) for a in range(groups)]
                for g, piece in enumerate(turn_lanes(pieces)):
                    wide[g, k, 8 * full + row, start : start + 16, :] = piece
            return 0

        if spare:
            lax.fori_loop(0, spare, widen_spare, 0)
    land()

    def turned(block):
        return jnp.transpose(block.reshape(peers * third, 128).astype(jnp.float32))

    first, second = turned(arrived[:, :third, :]), turned(arrived[:, third:, :])

    def collect(first, second, pick):
        extra = jnp.concatenate([first[width : width + half], second[width : width + half]], axis=0)
        parts = [first[:width], second[:width], extra]
        return parts, pick

    parts, _ = collect(first, second, pick_recv)
    line = sum(nn(parts[t].astype(jnp.bfloat16), pick_recv[t]) for t in range(3))

    for k in range(segment):
        line_rows[k] = line[:, k * lines : (k + 1) * lines].astype(jnp.bfloat16)
    for k in range(segment):
        inv_loads[k].wait()
        vector = line_rows[k].astype(jnp.float32)

        def force(b, _, k=k, vector=vector):
            base = pl.multiple_of(b * 8, 8)
            forcing[k, pl.ds(base, 8), :] = block_rows(inv, k, base, vector)
            return 0

        lax.fori_loop(0, blocks, force, 0)

    held = full + (spare > 0)
    for k in range(segment):
        packed = to_groups([forcing[k, 8 * b : 8 * b + 8, :] for b in range(blocks)], groups)
        for g in range(groups):
            for b in range(held):
                parts_in[g, k, 8 * b : 8 * b + 8, :] = packed[g][b]

    @pl.when(circ == 0)
    def _():
        inbox[0] = jnp.zeros_like(inbox[0])

    def hop(turn, slot, group):
        return pltpu.make_async_remote_copy(
            src_ref=outbox.at[turn, group],
            dst_ref=inbox.at[slot, group],
            send_sem=send_sem.at[turn, group],
            recv_sem=recv_sem.at[slot, group],
            device_id={"circ": right},
            device_id_type=MESH,
        )

    def visit(order, _):
        turn, group = order // groups, lax.rem(order, groups)

        @pl.when(circ + turn > 0)
        def _():
            hop(0, turn, group).wait_recv()

        rows = [inbox[turn, group, 8 * b : 8 * b + 8, :] for b in range(held)]
        for k in range(segment):
            add = [parts_in[group, k, 8 * b : 8 * b + 8, :] for b in range(held)]
            rows = advance(wide, group, k, replicate(rows, width, groups), add, width, groups)
            for b in range(held):
                solved[group, k, 8 * b : 8 * b + 8, :] = rows[b]
        for b in range(held):
            outbox[turn, group, 8 * b : 8 * b + 8, :] = rows[b]

        @pl.when(circ + turn < n_circ)
        def _():
            hop(turn, jnp.where(circ == n_circ - 1, 1, turn), group).start()

        return 0

    lax.fori_loop(0, 2 * groups, visit, 0)

    table = jnp.concatenate(
        [
            jnp.concatenate(
                from_groups(
                    [[solved[g, k, 8 * b : 8 * b + 8, :] for b in range(held)] for g in range(groups)], width
                ),
                axis=0,
            )
            for k in range(segment)
        ],
        axis=1,
    )
    whole, low, high = [jnp.concatenate(split(w), axis=0) for w in spread(table)]

    def both(picked):
        return picked[:, :128] + picked[:, 128:]

    lane = lax.broadcasted_iota(jnp.int32, (peers * third, 128), 1)
    first = both(nt(pick_recv[0], whole) + nt(pick_recv[2], low))
    second = both(nt(pick_recv[1], whole) + nt(pick_recv[2], high))
    back_sent[:, :third, :] = code(first, lane, width, half).reshape(peers, third, 128)
    back_sent[:, third:, :] = code(second, lane, width, half).reshape(peers, third, 128)
    start, land, drain_back = exchange(back_sent, back_arrived, back_send, back_recv)
    start()
    back_arrived[me] = back_sent[me]
    land()

    def opened(block):
        return jnp.transpose(decode(block.reshape(peers * third, 128), lane, width, half))

    first, second = opened(back_arrived[:, :third, :]), opened(back_arrived[:, third:, :])
    parts, _ = collect(first, second, pick_send)
    total = sum(nn(jnp.concatenate(split(parts[t]), axis=0), pick_send[t]) for t in range(3))
    out_ref[...] = total[:width] + total[width:]

    def sent_on(order, _):
        turn, group = order // groups, lax.rem(order, groups)

        @pl.when(circ + turn < n_circ)
        def _():
            hop(turn, 0, group).wait_send()

        return 0

    lax.fori_loop(0, 2 * groups, sent_on, 0)
    drain_go()
    drain_back()


def fused(elem_rows, coupling, inverses, send_rows, recv_cells, slot_counts):
    segment, width, _, lines = coupling.shape
    peers, slots = send_rows.shape[1], send_rows.shape[2]
    n_circ, n_span = lax.axis_size("circ"), lax.axis_size("span")
    third = slots // 3
    vmem = pl.BlockSpec(memory_space=pltpu.VMEM)
    hbm = pl.BlockSpec(memory_space=pl.ANY)
    groups = GROUPS
    full, spare = row_plan(width, groups)
    rows = 8 * (full + (spare > 0))
    boxes = pltpu.VMEM((2, groups, rows, lines), jnp.float32)
    packed = pltpu.VMEM((groups, segment, rows, lines), jnp.float32)
    pick = pltpu.VMEM((3, peers * third, segment * lines), jnp.bfloat16)
    go = pltpu.VMEM((peers, 2 * third, 128), jnp.bfloat16)
    back = pltpu.VMEM((peers, 2 * third, 128), jnp.int16)
    dma = pltpu.SemaphoreType.DMA
    return pl.pallas_call(
        functools.partial(fused_kernel, n_circ, n_span, groups),
        out_shape=jax.ShapeDtypeStruct(elem_rows.shape, jnp.float32),
        in_specs=[vmem, vmem, vmem, vmem, hbm, hbm],
        out_specs=vmem,
        scratch_shapes=[
            pltpu.VMEM(inverses.shape, jnp.bfloat16),
            pltpu.VMEM(coupling.shape, jnp.bfloat16),
            pltpu.VMEM((groups, segment, 8 * full + spare, width, lines), jnp.float32),
            pltpu.VMEM((segment, width, lines), jnp.bfloat16),
            pltpu.VMEM((segment, width, lines), jnp.float32),
            packed,
            packed,
            boxes,
            boxes,
            pick,
            pick,
            go,
            go,
            back,
            back,
            dma((segment,)),
            dma((segment,)),
            dma((2, groups)),
            dma((2, groups)),
            dma((peers,)),
            dma((peers,)),
            dma((peers,)),
            dma((peers,)),
        ],
        compiler_params=pltpu.CompilerParams(
            collective_id=1, has_side_effects=True, vmem_limit_bytes=60 * 1024 * 1024
        ),
        name="smooth",
    )(elem_rows, send_rows[0], recv_cells[0], slot_counts, inverses, coupling)


def packs(width, slots, cells, lines):
    return slots % 48 == 0 and width % 16 == 0 and width + width // 2 + 2 <= 128 and lines == 128


def local(*arrays):
    coupling, send_rows = arrays[1], arrays[3]
    if packs(coupling.shape[1], send_rows.shape[2], arrays[0].shape[1], coupling.shape[3]):
        return fused(*arrays)
    return staged(*arrays)


def solution(mesh):
    return jax.shard_map(
        local,
        mesh=mesh,
        in_specs=(
            P(None, ("circ", "span")),
            P("circ", None, None, "span"),
            P("circ", None, None, "span"),
            P(("circ", "span"), None, None),
            P(("circ", "span"), None, None),
            P(("circ", "span"), None),
        ),
        out_specs=P(None, ("circ", "span")),
        check_vma=False,
    )
```

```python
import functools

import jax
import jax.numpy as jnp
from jax import lax
from jax.experimental import pallas as pl
from jax.experimental.pallas import tpu as pltpu
from jax.sharding import PartitionSpec as P

MESH = pl.DeviceIdType.MESH


def merge(low, high, half, mask):
    if 2 * half == low.shape[0]:
        return jnp.where(mask, low, high) + pltpu.roll(jnp.where(mask, high, low), half, axis=0)
    back = low.shape[0] - half
    return jnp.where(mask, low + pltpu.roll(low, back, axis=0), high + pltpu.roll(high, half, axis=0))


def fold(parts):
    row = lax.broadcasted_iota(jnp.int32, parts[0].shape, 0)
    half = len(parts) // 2
    while half:
        mask = (row & half) == 0
        parts = [merge(parts[i], parts[i + half], half, mask) for i in range(half)]
        half //= 2
    return parts[0]


def block_rows(mat_ref, position, base, vector):
    width = vector.shape[0]
    parts = []
    for i in range(8):
        total = None
        for start in range(0, width, 16):
            piece = mat_ref[position, base + i, start : start + 16, :]
            term = piece.astype(jnp.float32) * vector[start : start + 16]
            total = term if total is None else total + term
        parts.append(total[:8] + total[8:])
    return fold(parts)


def relay_kernel(
    n_circ, rows_ref, inv_hbm, coup_hbm, out_ref, inv, coup, forcing, state, inbox, outbox, inv_sem, coup_sem, send_sem, recv_sem
):
    me = lax.axis_index("circ")
    right, left = lax.rem(me + 1, n_circ), lax.rem(me + n_circ - 1, n_circ)
    segment, width = coup.shape[0], coup.shape[1]
    blocks = width // 8

    loads = [pltpu.make_async_copy(inv_hbm.at[k], inv.at[k], inv_sem.at[k]) for k in range(segment)]
    loads += [pltpu.make_async_copy(coup_hbm.at[k], coup.at[k], coup_sem.at[k]) for k in range(segment)]
    for load in loads:
        load.start()

    barrier = pltpu.get_barrier_semaphore()
    for neighbour in (left, right):
        pl.semaphore_signal(barrier, inc=1, device_id={"circ": neighbour}, device_id_type=MESH)
    pl.semaphore_wait(barrier, 2)

    for k in range(segment):
        loads[k].wait()
        vector = rows_ref[k].astype(jnp.float32)

        def force(b, _, k=k, vector=vector):
            base = pl.multiple_of(b * 8, 8)
            forcing[k, pl.ds(base, 8), :] = block_rows(inv, k, base, vector)
            return 0

        lax.fori_loop(0, blocks, force, 0)
    for k in range(segment):
        loads[segment + k].wait()

    def hop(turn, slot):
        return pltpu.make_async_remote_copy(
            src_ref=outbox.at[turn],
            dst_ref=inbox.at[slot],
            send_sem=send_sem.at[turn],
            recv_sem=recv_sem.at[slot],
            device_id={"circ": right},
            device_id_type=MESH,
        )

    def sweep(target):
        def step(k, _):
            vector = state[...]

            def advance(b, _):
                base = pl.multiple_of(b * 8, 8)
                value = forcing[k, pl.ds(base, 8), :] + block_rows(coup, k, base, vector)
                state[pl.ds(base, 8), :] = value
                if target is not None:
                    target[k, pl.ds(base, 8), :] = value
                return 0

            lax.fori_loop(0, blocks, advance, 0)
            return 0

        lax.fori_loop(0, segment, step, 0)

    @pl.when(me == 0)
    def _():
        state[...] = jnp.zeros_like(state)

    @pl.when(me > 0)
    def _():
        hop(0, 0).wait_recv()
        state[...] = inbox[0]

    sweep(None)
    outbox[0] = state[...]
    slot = jnp.where(me == n_circ - 1, 1, 0)
    first = hop(0, slot)
    first.start()
    hop(0, 1).wait_recv()
    state[...] = inbox[1]
    sweep(out_ref)

    @pl.when(me < n_circ - 1)
    def _():
        outbox[1] = state[...]
        second = hop(1, 1)
        second.start()
        second.wait_send()

    first.wait_send()


def relay(rows, inverses, coupling):
    segment, width, _, lines = coupling.shape
    n_circ = lax.axis_size("circ")
    state = pltpu.VMEM((width, lines), jnp.float32)
    boxes = pltpu.VMEM((2, width, lines), jnp.float32)
    return pl.pallas_call(
        functools.partial(relay_kernel, n_circ),
        out_shape=jax.ShapeDtypeStruct((segment, width, lines), jnp.float32),
        in_specs=[
            pl.BlockSpec(memory_space=pltpu.VMEM),
            pl.BlockSpec(memory_space=pl.ANY),
            pl.BlockSpec(memory_space=pl.ANY),
        ],
        out_specs=pl.BlockSpec(memory_space=pltpu.VMEM),
        scratch_shapes=[
            pltpu.VMEM(inverses.shape, jnp.bfloat16),
            pltpu.VMEM(coupling.shape, jnp.bfloat16),
            pltpu.VMEM((segment, width, lines), jnp.float32),
            state,
            boxes,
            boxes,
            pltpu.SemaphoreType.DMA((segment,)),
            pltpu.SemaphoreType.DMA((segment,)),
            pltpu.SemaphoreType.DMA((2,)),
            pltpu.SemaphoreType.DMA((2,)),
        ],
        compiler_params=pltpu.CompilerParams(
            collective_id=0, has_side_effects=True, vmem_limit_bytes=48 * 1024 * 1024
        ),
        name="relay",
    )(rows, inverses, coupling)


def staged(elem_rows, coupling, inverses, send_rows, recv_cells, slot_counts):
    features, cell_count = elem_rows.shape
    peer_count, slot_count = (send_rows.shape[1], send_rows.shape[2])
    segment, line_count = (coupling.shape[0], coupling.shape[3])
    outgoing = jnp.take(elem_rows, send_rows[0].reshape(-1), axis=1).reshape(
        features, peer_count, slot_count
    )
    arrived = lax.all_to_all(outgoing, ("circ", "span"), split_axis=1, concat_axis=1, tiled=True)
    filled = jnp.arange(slot_count, dtype=jnp.int32)[None, :] < slot_counts[0][:, None]
    targets = jnp.where(filled, recv_cells[0], cell_count).reshape(-1)
    line_rows = (
        jnp.zeros((features, cell_count), jnp.bfloat16)
        .at[:, targets]
        .set(arrived.reshape(features, -1), mode="drop")
    )
    line_cells = jnp.transpose(line_rows.reshape(features, segment, line_count), (1, 0, 2))
    states = relay(line_cells, inverses, coupling)
    solved = jnp.transpose(states, (1, 0, 2)).reshape(features, cell_count)
    returning = jnp.take(solved, recv_cells[0].reshape(-1), axis=1).reshape(
        features, peer_count, slot_count
    )
    returning = jnp.where(filled[None, :, :], returning, 0.0)
    returned = lax.all_to_all(returning, ("circ", "span"), split_axis=1, concat_axis=1, tiled=True)
    return (
        jnp.zeros((features, cell_count), jnp.float32)
        .at[:, send_rows[0].reshape(-1)]
        .add(returned.reshape(features, -1))
    )


def code(values, lane, width, extra):
    size = jnp.abs(values)
    tiny = jnp.float32(1e-36)
    top_main = jnp.max(jnp.where(lane < width, size, tiny), axis=1, keepdims=True)
    top_extra = jnp.max(jnp.where(lane < width, tiny, size), axis=1, keepdims=True)
    power_main = jnp.ceil(jnp.log2(jnp.maximum(top_main, tiny)))
    power_extra = jnp.ceil(jnp.log2(jnp.maximum(top_extra, tiny)))
    root = jnp.exp2(-0.5 * jnp.where(lane < width, power_main, power_extra))
    whole = jnp.round(values * root * root * 32000.0)
    whole = jnp.where(lane == width + extra, power_main, whole)
    whole = jnp.where(lane == width + extra + 1, power_extra, whole)
    return whole.astype(jnp.int32).astype(jnp.int16)


def decode(coded, lane, width, extra):
    whole = coded.astype(jnp.int32).astype(jnp.float32)
    power_main = jnp.sum(jnp.where(lane == width + extra, whole, 0.0), axis=1, keepdims=True)
    power_extra = jnp.sum(jnp.where(lane == width + extra + 1, whole, 0.0), axis=1, keepdims=True)
    root = jnp.exp2(0.5 * jnp.where(lane < width, power_main, power_extra))
    return jnp.where(lane < width + extra, whole * (1.0 / 32000.0) * root * root, 0.0)


def split(values):
    high = values.astype(jnp.bfloat16)
    return high, (values - high.astype(jnp.float32)).astype(jnp.bfloat16)


def nt(a, b):
    return lax.dot_general(a, b, (((1,), (1,)), ((), ())), preferred_element_type=jnp.float32)


def nn(a, b):
    return jnp.dot(a, b, preferred_element_type=jnp.float32)


def spread(table):
    width, cells = table.shape
    half = width // 2
    head = jnp.zeros((width, cells), jnp.float32)
    tail = jnp.zeros((128 - width - half, cells), jnp.float32)
    return (
        jnp.concatenate([table, jnp.zeros((128 - width, cells), jnp.float32)], axis=0),
        jnp.concatenate([head, table[:half], tail], axis=0),
        jnp.concatenate([head, table[half:], tail], axis=0),
    )


def flip_block(source, target, flat, position, block):
    width = source.shape[2]
    for i in range(16):
        for start in range(0, width, 16):
            piece = source[position, block * 16 + i, start : start + 16, :].astype(jnp.float32)
            flat[(width + 8) * i + start : (width + 8) * i + start + 16, :] = piece
    rows = pl.ds(pl.multiple_of(block * 16, 16), 16)
    for j in range(width):
        target[position, j, rows, :] = flat[pl.ds(j, 16, stride=width + 8), :].astype(jnp.bfloat16)


def columns(matrix, position, planes, spots):
    width, count = planes.shape[1], planes.shape[0]

    def run(tile, first, last):
        total = None
        for j in range(first, last):
            for p in range(count):
                spot = spots[p, j].astype(jnp.float32)
                term = matrix[position, j, 16 * tile : 16 * tile + 16, :].astype(jnp.float32) * spot
                total = term if total is None else total + term
        return total

    for j in range(width):
        for p in range(count):
            spots[p, j] = jnp.broadcast_to(planes[p, j : j + 1, :], (16, planes.shape[2])).astype(jnp.bfloat16)
    tiles = width // 16
    whole = tiles // 4 * 4
    totals = [run(tile, 0, width) for tile in range(whole)]
    for tile in range(whole, tiles):
        cuts = [width * q // 4 for q in range(5)]
        quarters = [run(tile, cuts[q], cuts[q + 1]) for q in range(4)]
        totals.append((quarters[0] + quarters[1]) + (quarters[2] + quarters[3]))
    return jnp.concatenate(totals, axis=0)


def fused_kernel(
    n_circ, n_span, elem_ref, send_ref, recv_ref, count_ref, inv_hbm, coup_hbm, out_ref,
    inv, coup, wide, flat, planes, spots, line_rows, forcing, solved, state, inbox, pick_send, pick_recv, sent, arrived, back_sent, back_arrived,
    inv_sem, coup_sem, send_sem, recv_sem, go_send, go_recv, back_send, back_recv,
):
    circ, span = lax.axis_index("circ"), lax.axis_index("span")
    peers = n_circ * n_span
    me = circ * n_span + span
    right = lax.rem(circ + 1, n_circ)
    segment, width, lines = forcing.shape
    cells = segment * lines
    third = sent.shape[1] // 2
    half = width // 2
    blocks = width // 8

    coup_loads = [pltpu.make_async_copy(coup_hbm.at[k], coup.at[k], coup_sem.at[k]) for k in range(segment)]
    inv_loads = [pltpu.make_async_copy(inv_hbm.at[k], inv.at[k], inv_sem.at[k]) for k in range(segment)]
    for load in coup_loads + inv_loads:
        load.start()

    barrier = pltpu.get_barrier_semaphore()

    def greet(o, _):
        peer = lax.rem(me + o, peers)
        pl.semaphore_signal(
            barrier, inc=1, device_id={"circ": peer // n_span, "span": peer % n_span}, device_id_type=MESH
        )
        return 0

    lax.fori_loop(1, peers, greet, 0)

    def build(index_ref, pick, masked):
        lane = lax.broadcasted_iota(jnp.int32, (third, index_ref.shape[1]), 1)
        slot = lax.broadcasted_iota(jnp.int32, (third, index_ref.shape[1]), 0)
        number = lax.broadcasted_iota(jnp.int32, (third, cells), 1).astype(jnp.float32)
        owner = lax.broadcasted_iota(jnp.int32, count_ref.shape, 1)
        rank = lax.broadcasted_iota(jnp.int32, (third, 1), 0).astype(jnp.float32)

        def one(p, _):
            row = index_ref[pl.ds(p, 1), :].astype(jnp.float32)
            if masked:
                counts = count_ref[...].astype(jnp.float32)
                count = jnp.sum(jnp.where(owner == p, counts, 0.0), axis=1, keepdims=True)
            for t in range(3):
                column = jnp.sum(jnp.where(lane == slot + t * third, row, 0.0), axis=1, keepdims=True)
                if masked:
                    column = jnp.where(rank + float(t * third) < count, column, -1.0)
                hot = jnp.where(number == column, 1.0, 0.0).astype(jnp.bfloat16)
                pick[t, pl.ds(pl.multiple_of(p * third, third), third), :] = hot
            return 0

        lax.fori_loop(0, peers, one, 0)

    def exchange(outs, ins, outs_sem, ins_sem):
        def copy(peer, landing):
            return pltpu.make_async_remote_copy(
                src_ref=outs.at[peer],
                dst_ref=ins.at[landing],
                send_sem=outs_sem.at[peer],
                recv_sem=ins_sem.at[landing],
                device_id={"circ": peer // n_span, "span": peer % n_span},
                device_id_type=MESH,
            )

        def start(o, _):
            copy(lax.rem(me + o, peers), me).start()
            return 0

        def land(o, _):
            peer = lax.rem(me + peers - o, peers)
            copy(peer, peer).wait_recv()
            return 0

        def drain(o, _):
            copy(lax.rem(me + o, peers), me).wait_send()
            return 0

        return (
            lambda: lax.fori_loop(1, peers, start, 0),
            lambda: lax.fori_loop(1, peers, land, 0),
            lambda: lax.fori_loop(1, peers, drain, 0),
        )

    build(send_ref, pick_send, False)
    whole, low, high = [w.astype(jnp.bfloat16) for w in spread(elem_ref[...].astype(jnp.float32))]
    first = nt(pick_send[0], whole) + nt(pick_send[2], low)
    second = nt(pick_send[1], whole) + nt(pick_send[2], high)
    sent[:, :third, :] = first.astype(jnp.bfloat16).reshape(peers, third, 128)
    sent[:, third:, :] = second.astype(jnp.bfloat16).reshape(peers, third, 128)

    pl.semaphore_wait(barrier, peers - 1)
    start, land, drain_go = exchange(sent, arrived, go_send, go_recv)
    start()
    arrived[me] = sent[me]
    build(recv_ref, pick_recv, True)
    for k in range(segment):
        coup_loads[k].wait()

        def widen(b, _, k=k):
            flip_block(coup, wide, flat, k, b)
            return 0

        lax.fori_loop(0, width // 16, widen, 0)
    land()

    def turned(block):
        return jnp.transpose(block.reshape(peers * third, 128).astype(jnp.float32))

    first, second = turned(arrived[:, :third, :]), turned(arrived[:, third:, :])

    def collect(first, second, pick):
        extra = jnp.concatenate([first[width : width + half], second[width : width + half]], axis=0)
        parts = [first[:width], second[:width], extra]
        return parts, pick

    parts, _ = collect(first, second, pick_recv)
    line = sum(nn(parts[t].astype(jnp.bfloat16), pick_recv[t]) for t in range(3))

    for k in range(segment):
        line_rows[k] = line[:, k * lines : (k + 1) * lines].astype(jnp.bfloat16)
    for k in range(segment):
        inv_loads[k].wait()
        vector = line_rows[k].astype(jnp.float32)

        def force(b, _, k=k, vector=vector):
            base = pl.multiple_of(b * 8, 8)
            forcing[k, pl.ds(base, 8), :] = block_rows(inv, k, base, vector)
            return 0

        lax.fori_loop(0, blocks, force, 0)

    cut = (blocks // 4) * 16
    chunks = ((0, cut), (cut, width))

    def hop(turn, slot, chunk):
        rows = pl.ds(chunks[chunk][0], chunks[chunk][1] - chunks[chunk][0])
        return pltpu.make_async_remote_copy(
            src_ref=solved.at[segment - 1, rows],
            dst_ref=inbox.at[slot, rows],
            send_sem=send_sem.at[turn, chunk],
            recv_sem=recv_sem.at[slot, chunk],
            device_id={"circ": right},
            device_id_type=MESH,
        )

    def sweep(emit):
        value = state[...]
        for k in range(segment):
            high, low = split(value)
            planes[0] = high.astype(jnp.float32)
            planes[1] = low.astype(jnp.float32)
            value = forcing[k] + columns(wide, k, planes, spots)
            solved[k] = value
        for chunk in range(2):
            emit(chunk)

    @pl.when(circ == 0)
    def _():
        state[...] = jnp.zeros_like(state)

    @pl.when(circ > 0)
    def _():
        for chunk in range(2):
            hop(0, 0, chunk).wait_recv()
        state[...] = inbox[0]

    landing = jnp.where(circ == n_circ - 1, 1, 0)
    sweep(lambda chunk: hop(0, landing, chunk).start())
    for chunk in range(2):
        hop(0, 1, chunk).wait_send()
    for chunk in range(2):
        hop(0, 1, chunk).wait_recv()
    state[...] = inbox[1]

    def last(chunk):
        @pl.when(circ < n_circ - 1)
        def _():
            hop(1, 1, chunk).start()

    sweep(last)

    table = jnp.concatenate([solved[k] for k in range(segment)], axis=1)
    whole, low, high = [jnp.concatenate(split(w), axis=0) for w in spread(table)]

    def both(picked):
        return picked[:, :128] + picked[:, 128:]

    lane = lax.broadcasted_iota(jnp.int32, (peers * third, 128), 1)
    first = both(nt(pick_recv[0], whole) + nt(pick_recv[2], low))
    second = both(nt(pick_recv[1], whole) + nt(pick_recv[2], high))
    back_sent[:, :third, :] = code(first, lane, width, half).reshape(peers, third, 128)
    back_sent[:, third:, :] = code(second, lane, width, half).reshape(peers, third, 128)
    start, land, drain_back = exchange(back_sent, back_arrived, back_send, back_recv)
    start()
    back_arrived[me] = back_sent[me]
    land()

    def opened(block):
        return jnp.transpose(decode(block.reshape(peers * third, 128), lane, width, half))

    first, second = opened(back_arrived[:, :third, :]), opened(back_arrived[:, third:, :])
    parts, _ = collect(first, second, pick_send)
    total = sum(nn(jnp.concatenate(split(parts[t]), axis=0), pick_send[t]) for t in range(3))
    out_ref[...] = total[:width] + total[width:]

    @pl.when(circ < n_circ - 1)
    def _():
        for chunk in range(2):
            hop(1, 1, chunk).wait_send()

    drain_go()
    drain_back()


def fused(elem_rows, coupling, inverses, send_rows, recv_cells, slot_counts):
    segment, width, _, lines = coupling.shape
    peers, slots = send_rows.shape[1], send_rows.shape[2]
    n_circ, n_span = lax.axis_size("circ"), lax.axis_size("span")
    third = slots // 3
    vmem = pl.BlockSpec(memory_space=pltpu.VMEM)
    hbm = pl.BlockSpec(memory_space=pl.ANY)
    boxes = pltpu.VMEM((2, width, lines), jnp.float32)
    states = pltpu.VMEM((segment, width, lines), jnp.float32)
    pick = pltpu.VMEM((3, peers * third, segment * lines), jnp.bfloat16)
    go = pltpu.VMEM((peers, 2 * third, 128), jnp.bfloat16)
    back = pltpu.VMEM((peers, 2 * third, 128), jnp.int16)
    dma = pltpu.SemaphoreType.DMA
    return pl.pallas_call(
        functools.partial(fused_kernel, n_circ, n_span),
        out_shape=jax.ShapeDtypeStruct(elem_rows.shape, jnp.float32),
        in_specs=[vmem, vmem, vmem, vmem, hbm, hbm],
        out_specs=vmem,
        scratch_shapes=[
            pltpu.VMEM(inverses.shape, jnp.bfloat16),
            pltpu.VMEM(coupling.shape, jnp.bfloat16),
            pltpu.VMEM(coupling.shape, jnp.bfloat16),
            pltpu.VMEM((16 * (width + 8), lines), jnp.float32),
            pltpu.VMEM((2, width, lines), jnp.float32),
            pltpu.VMEM((2, width, 16, lines), jnp.bfloat16),
            pltpu.VMEM((segment, width, lines), jnp.bfloat16),
            states,
            states,
            pltpu.VMEM((width, lines), jnp.float32),
            boxes,
            pick,
            pick,
            go,
            go,
            back,
            back,
            dma((segment,)),
            dma((segment,)),
            dma((2, 2)),
            dma((2, 2)),
            dma((peers,)),
            dma((peers,)),
            dma((peers,)),
            dma((peers,)),
        ],
        compiler_params=pltpu.CompilerParams(
            collective_id=1, has_side_effects=True, vmem_limit_bytes=60 * 1024 * 1024
        ),
        name="smooth",
    )(elem_rows, send_rows[0], recv_cells[0], slot_counts, inverses, coupling)


def packs(width, slots, cells, lines):
    return slots % 48 == 0 and width % 16 == 0 and width + width // 2 + 2 <= 128 and lines == 128


def local(*arrays):
    coupling, send_rows = arrays[1], arrays[3]
    if packs(coupling.shape[1], send_rows.shape[2], arrays[0].shape[1], coupling.shape[3]):
        return fused(*arrays)
    return staged(*arrays)


def solution(mesh):
    return jax.shard_map(
        local,
        mesh=mesh,
        in_specs=(
            P(None, ("circ", "span")),
            P("circ", None, None, "span"),
            P("circ", None, None, "span"),
            P(("circ", "span"), None, None),
            P(("circ", "span"), None, None),
            P(("circ", "span"), None),
        ),
        out_specs=P(None, ("circ", "span")),
        check_vma=False,
    )
```

```python
import functools

import jax
import jax.numpy as jnp
from jax import lax
from jax.experimental import pallas as pl
from jax.experimental.pallas import tpu as pltpu
from jax.sharding import PartitionSpec as P

MESH = pl.DeviceIdType.MESH


def merge(low, high, half, mask):
    if 2 * half == low.shape[0]:
        return jnp.where(mask, low, high) + pltpu.roll(jnp.where(mask, high, low), half, axis=0)
    back = low.shape[0] - half
    return jnp.where(mask, low + pltpu.roll(low, back, axis=0), high + pltpu.roll(high, half, axis=0))


def fold(parts):
    row = lax.broadcasted_iota(jnp.int32, parts[0].shape, 0)
    half = len(parts) // 2
    while half:
        mask = (row & half) == 0
        parts = [merge(parts[i], parts[i + half], half, mask) for i in range(half)]
        half //= 2
    return parts[0]


def block_rows(mat_ref, position, base, vector):
    width = vector.shape[0]
    parts = []
    for i in range(8):
        total = None
        for start in range(0, width, 16):
            piece = mat_ref[position, base + i, start : start + 16, :]
            term = piece.astype(jnp.float32) * vector[start : start + 16]
            total = term if total is None else total + term
        parts.append(total[:8] + total[8:])
    return fold(parts)


def relay_kernel(
    n_circ, rows_ref, inv_hbm, coup_hbm, out_ref, inv, coup, forcing, state, inbox, outbox, inv_sem, coup_sem, send_sem, recv_sem
):
    me = lax.axis_index("circ")
    right, left = lax.rem(me + 1, n_circ), lax.rem(me + n_circ - 1, n_circ)
    segment, width = coup.shape[0], coup.shape[1]
    blocks = width // 8

    loads = [pltpu.make_async_copy(inv_hbm.at[k], inv.at[k], inv_sem.at[k]) for k in range(segment)]
    loads += [pltpu.make_async_copy(coup_hbm.at[k], coup.at[k], coup_sem.at[k]) for k in range(segment)]
    for load in loads:
        load.start()

    barrier = pltpu.get_barrier_semaphore()
    for neighbour in (left, right):
        pl.semaphore_signal(barrier, inc=1, device_id={"circ": neighbour}, device_id_type=MESH)
    pl.semaphore_wait(barrier, 2)

    for k in range(segment):
        loads[k].wait()
        vector = rows_ref[k].astype(jnp.float32)

        def force(b, _, k=k, vector=vector):
            base = pl.multiple_of(b * 8, 8)
            forcing[k, pl.ds(base, 8), :] = block_rows(inv, k, base, vector)
            return 0

        lax.fori_loop(0, blocks, force, 0)
    for k in range(segment):
        loads[segment + k].wait()

    def hop(turn, slot):
        return pltpu.make_async_remote_copy(
            src_ref=outbox.at[turn],
            dst_ref=inbox.at[slot],
            send_sem=send_sem.at[turn],
            recv_sem=recv_sem.at[slot],
            device_id={"circ": right},
            device_id_type=MESH,
        )

    def sweep(target):
        def step(k, _):
            vector = state[...]

            def advance(b, _):
                base = pl.multiple_of(b * 8, 8)
                value = forcing[k, pl.ds(base, 8), :] + block_rows(coup, k, base, vector)
                state[pl.ds(base, 8), :] = value
                if target is not None:
                    target[k, pl.ds(base, 8), :] = value
                return 0

            lax.fori_loop(0, blocks, advance, 0)
            return 0

        lax.fori_loop(0, segment, step, 0)

    @pl.when(me == 0)
    def _():
        state[...] = jnp.zeros_like(state)

    @pl.when(me > 0)
    def _():
        hop(0, 0).wait_recv()
        state[...] = inbox[0]

    sweep(None)
    outbox[0] = state[...]
    slot = jnp.where(me == n_circ - 1, 1, 0)
    first = hop(0, slot)
    first.start()
    hop(0, 1).wait_recv()
    state[...] = inbox[1]
    sweep(out_ref)

    @pl.when(me < n_circ - 1)
    def _():
        outbox[1] = state[...]
        second = hop(1, 1)
        second.start()
        second.wait_send()

    first.wait_send()


def relay(rows, inverses, coupling):
    segment, width, _, lines = coupling.shape
    n_circ = lax.axis_size("circ")
    state = pltpu.VMEM((width, lines), jnp.float32)
    boxes = pltpu.VMEM((2, width, lines), jnp.float32)
    return pl.pallas_call(
        functools.partial(relay_kernel, n_circ),
        out_shape=jax.ShapeDtypeStruct((segment, width, lines), jnp.float32),
        in_specs=[
            pl.BlockSpec(memory_space=pltpu.VMEM),
            pl.BlockSpec(memory_space=pl.ANY),
            pl.BlockSpec(memory_space=pl.ANY),
        ],
        out_specs=pl.BlockSpec(memory_space=pltpu.VMEM),
        scratch_shapes=[
            pltpu.VMEM(inverses.shape, jnp.bfloat16),
            pltpu.VMEM(coupling.shape, jnp.bfloat16),
            pltpu.VMEM((segment, width, lines), jnp.float32),
            state,
            boxes,
            boxes,
            pltpu.SemaphoreType.DMA((segment,)),
            pltpu.SemaphoreType.DMA((segment,)),
            pltpu.SemaphoreType.DMA((2,)),
            pltpu.SemaphoreType.DMA((2,)),
        ],
        compiler_params=pltpu.CompilerParams(
            collective_id=0, has_side_effects=True, vmem_limit_bytes=48 * 1024 * 1024
        ),
        name="relay",
    )(rows, inverses, coupling)


def staged(elem_rows, coupling, inverses, send_rows, recv_cells, slot_counts):
    features, cell_count = elem_rows.shape
    peer_count, slot_count = (send_rows.shape[1], send_rows.shape[2])
    segment, line_count = (coupling.shape[0], coupling.shape[3])
    outgoing = jnp.take(elem_rows, send_rows[0].reshape(-1), axis=1).reshape(
        features, peer_count, slot_count
    )
    arrived = lax.all_to_all(outgoing, ("circ", "span"), split_axis=1, concat_axis=1, tiled=True)
    filled = jnp.arange(slot_count, dtype=jnp.int32)[None, :] < slot_counts[0][:, None]
    targets = jnp.where(filled, recv_cells[0], cell_count).reshape(-1)
    line_rows = (
        jnp.zeros((features, cell_count), jnp.bfloat16)
        .at[:, targets]
        .set(arrived.reshape(features, -1), mode="drop")
    )
    line_cells = jnp.transpose(line_rows.reshape(features, segment, line_count), (1, 0, 2))
    states = relay(line_cells, inverses, coupling)
    solved = jnp.transpose(states, (1, 0, 2)).reshape(features, cell_count)
    returning = jnp.take(solved, recv_cells[0].reshape(-1), axis=1).reshape(
        features, peer_count, slot_count
    )
    returning = jnp.where(filled[None, :, :], returning, 0.0)
    returned = lax.all_to_all(returning, ("circ", "span"), split_axis=1, concat_axis=1, tiled=True)
    return (
        jnp.zeros((features, cell_count), jnp.float32)
        .at[:, send_rows[0].reshape(-1)]
        .add(returned.reshape(features, -1))
    )


def code(table):
    top = jnp.max(jnp.abs(table), axis=0, keepdims=True)
    power = jnp.ceil(jnp.log2(jnp.maximum(top, jnp.float32(1e-36))))
    root = jnp.exp2(-0.5 * power)
    whole = jnp.round(table * root * root * 32000.0)
    upper = jnp.round(whole * (1.0 / 256.0))
    return upper, whole - 256.0 * upper, power


def placed(table, power):
    parts = spread(table)
    width, cells = table.shape
    start = width + width // 2
    row = lax.broadcasted_iota(jnp.int32, (8, cells), 0)
    marks = [jnp.where(row == spot, power, 0.0) for spot in (0, 1, 1)]
    return [jnp.concatenate([part[:start], mark], axis=0) for part, mark in zip(parts, marks)]


def decode(whole, marks, spot):
    upper = jnp.round(whole * (1.0 / 256.0))
    row = lax.broadcasted_iota(jnp.int32, marks.shape, 0)
    power = jnp.where(row == spot, marks, 0.0)
    return jnp.concatenate([upper, whole - 256.0 * upper, power, jnp.zeros_like(power)], axis=0).astype(jnp.bfloat16)


def split(values):
    high = values.astype(jnp.bfloat16)
    return high, (values - high.astype(jnp.float32)).astype(jnp.bfloat16)


def nt(a, b):
    return lax.dot_general(a, b, (((1,), (1,)), ((), ())), preferred_element_type=jnp.float32)


def nn(a, b):
    return jnp.dot(a, b, preferred_element_type=jnp.float32)


def spread(table):
    width, cells = table.shape
    half = width // 2
    head = jnp.zeros((width, cells), jnp.float32)
    tail = jnp.zeros((128 - width - half, cells), jnp.float32)
    return (
        jnp.concatenate([table, jnp.zeros((128 - width, cells), jnp.float32)], axis=0),
        jnp.concatenate([head, table[:half], tail], axis=0),
        jnp.concatenate([head, table[half:], tail], axis=0),
    )


def flip_block(source, target, flat, position, block):
    width = source.shape[2]
    for i in range(16):
        for start in range(0, width, 16):
            piece = source[position, block * 16 + i, start : start + 16, :].astype(jnp.float32)
            flat[(width + 8) * i + start : (width + 8) * i + start + 16, :] = piece
    rows = pl.ds(pl.multiple_of(block * 16, 16), 16)
    for j in range(width):
        target[position, j, rows, :] = flat[pl.ds(j, 16, stride=width + 8), :].astype(jnp.bfloat16)


def columns(matrix, position, planes, spots):
    width, count = planes.shape[1], planes.shape[0]

    def run(tile, first, last):
        total = None
        for j in range(first, last):
            for p in range(count):
                spot = spots[p, j].astype(jnp.float32)
                term = matrix[position, j, 16 * tile : 16 * tile + 16, :].astype(jnp.float32) * spot
                total = term if total is None else total + term
        return total

    for j in range(width):
        for p in range(count):
            spots[p, j] = jnp.broadcast_to(planes[p, j : j + 1, :], (16, planes.shape[2])).astype(jnp.bfloat16)
    tiles = width // 16
    whole = tiles // 4 * 4
    totals = [run(tile, 0, width) for tile in range(whole)]
    for tile in range(whole, tiles):
        cuts = [width * q // 4 for q in range(5)]
        quarters = [run(tile, cuts[q], cuts[q + 1]) for q in range(4)]
        totals.append((quarters[0] + quarters[1]) + (quarters[2] + quarters[3]))
    return jnp.concatenate(totals, axis=0)


def fused_kernel(
    n_circ, n_span, elem_ref, send_ref, recv_ref, count_ref, inv_hbm, coup_hbm, out_ref,
    inv, coup, wide, flat, planes, spots, line_rows, forcing, solved, state, inbox, pick_send, pick_recv, sent, arrived, back_sent, back_arrived,
    inv_sem, coup_sem, send_sem, recv_sem, go_send, go_recv, back_send, back_recv,
):
    circ, span = lax.axis_index("circ"), lax.axis_index("span")
    peers = n_circ * n_span
    me = circ * n_span + span
    right = lax.rem(circ + 1, n_circ)
    segment, width, lines = forcing.shape
    cells = segment * lines
    third = sent.shape[1] // 2
    half = width // 2
    blocks = width // 8

    coup_loads = [pltpu.make_async_copy(coup_hbm.at[k], coup.at[k], coup_sem.at[k]) for k in range(segment)]
    inv_loads = [pltpu.make_async_copy(inv_hbm.at[k], inv.at[k], inv_sem.at[k]) for k in range(segment)]
    for load in coup_loads + inv_loads:
        load.start()

    barrier = pltpu.get_barrier_semaphore()

    def greet(o, _):
        peer = lax.rem(me + o, peers)
        pl.semaphore_signal(
            barrier, inc=1, device_id={"circ": peer // n_span, "span": peer % n_span}, device_id_type=MESH
        )
        return 0

    lax.fori_loop(1, peers, greet, 0)

    def build(index_ref, pick, masked):
        lane = lax.broadcasted_iota(jnp.int32, (third, index_ref.shape[1]), 1)
        slot = lax.broadcasted_iota(jnp.int32, (third, index_ref.shape[1]), 0)
        number = lax.broadcasted_iota(jnp.int32, (third, cells), 1).astype(jnp.float32)
        owner = lax.broadcasted_iota(jnp.int32, count_ref.shape, 1)
        rank = lax.broadcasted_iota(jnp.int32, (third, 1), 0).astype(jnp.float32)

        def one(p, _):
            row = index_ref[pl.ds(p, 1), :].astype(jnp.float32)
            if masked:
                counts = count_ref[...].astype(jnp.float32)
                count = jnp.sum(jnp.where(owner == p, counts, 0.0), axis=1, keepdims=True)
            for t in range(3):
                column = jnp.sum(jnp.where(lane == slot + t * third, row, 0.0), axis=1, keepdims=True)
                if masked:
                    column = jnp.where(rank + float(t * third) < count, column, -1.0)
                hot = jnp.where(number == column, 1.0, 0.0).astype(jnp.bfloat16)
                pick[t, pl.ds(pl.multiple_of(p * third, third), third), :] = hot
            return 0

        lax.fori_loop(0, peers, one, 0)

    def exchange(outs, ins, outs_sem, ins_sem):
        def copy(peer, landing):
            return pltpu.make_async_remote_copy(
                src_ref=outs.at[peer],
                dst_ref=ins.at[landing],
                send_sem=outs_sem.at[peer],
                recv_sem=ins_sem.at[landing],
                device_id={"circ": peer // n_span, "span": peer % n_span},
                device_id_type=MESH,
            )

        def start(o, _):
            copy(lax.rem(me + o, peers), me).start()
            return 0

        def land(o, _):
            peer = lax.rem(me + peers - o, peers)
            copy(peer, peer).wait_recv()
            return 0

        def drain(o, _):
            copy(lax.rem(me + o, peers), me).wait_send()
            return 0

        return (
            lambda: lax.fori_loop(1, peers, start, 0),
            lambda: lax.fori_loop(1, peers, land, 0),
            lambda: lax.fori_loop(1, peers, drain, 0),
        )

    build(send_ref, pick_send, False)
    whole, low, high = [w.astype(jnp.bfloat16) for w in spread(elem_ref[...].astype(jnp.float32))]
    first = nt(pick_send[0], whole) + nt(pick_send[2], low)
    second = nt(pick_send[1], whole) + nt(pick_send[2], high)
    sent[:, :third, :] = first.astype(jnp.bfloat16).reshape(peers, third, 128)
    sent[:, third:, :] = second.astype(jnp.bfloat16).reshape(peers, third, 128)

    pl.semaphore_wait(barrier, peers - 1)
    start, land, drain_go = exchange(sent, arrived, go_send, go_recv)
    start()
    arrived[me] = sent[me]
    build(recv_ref, pick_recv, True)
    for k in range(segment):
        coup_loads[k].wait()

        def widen(b, _, k=k):
            flip_block(coup, wide, flat, k, b)
            return 0

        lax.fori_loop(0, width // 16, widen, 0)
    land()

    def turned(block):
        return jnp.transpose(block.reshape(peers * third, 128).astype(jnp.float32))

    first, second = turned(arrived[:, :third, :]), turned(arrived[:, third:, :])

    def collect(first, second, pick):
        extra = jnp.concatenate([first[width : width + half], second[width : width + half]], axis=0)
        parts = [first[:width], second[:width], extra]
        return parts, pick

    parts, _ = collect(first, second, pick_recv)
    line = sum(nn(parts[t].astype(jnp.bfloat16), pick_recv[t]) for t in range(3))

    for k in range(segment):
        line_rows[k] = line[:, k * lines : (k + 1) * lines].astype(jnp.bfloat16)
    for k in range(segment):
        inv_loads[k].wait()
        vector = line_rows[k].astype(jnp.float32)

        def force(b, _, k=k, vector=vector):
            base = pl.multiple_of(b * 8, 8)
            forcing[k, pl.ds(base, 8), :] = block_rows(inv, k, base, vector)
            return 0

        lax.fori_loop(0, blocks, force, 0)

    cut = (blocks // 4) * 16
    chunks = ((0, cut), (cut, width))

    def hop(turn, slot, chunk):
        rows = pl.ds(chunks[chunk][0], chunks[chunk][1] - chunks[chunk][0])
        return pltpu.make_async_remote_copy(
            src_ref=solved.at[segment - 1, rows],
            dst_ref=inbox.at[slot, rows],
            send_sem=send_sem.at[turn, chunk],
            recv_sem=recv_sem.at[slot, chunk],
            device_id={"circ": right},
            device_id_type=MESH,
        )

    def sweep(emit):
        value = state[...]
        for k in range(segment):
            high, low = split(value)
            planes[0] = high.astype(jnp.float32)
            planes[1] = low.astype(jnp.float32)
            value = forcing[k] + columns(wide, k, planes, spots)
            solved[k] = value
        for chunk in range(2):
            emit(chunk)

    @pl.when(circ == 0)
    def _():
        state[...] = jnp.zeros_like(state)

    @pl.when(circ > 0)
    def _():
        for chunk in range(2):
            hop(0, 0, chunk).wait_recv()
        state[...] = inbox[0]

    landing = jnp.where(circ == n_circ - 1, 1, 0)
    sweep(lambda chunk: hop(0, landing, chunk).start())
    for chunk in range(2):
        hop(0, 1, chunk).wait_send()
    for chunk in range(2):
        hop(0, 1, chunk).wait_recv()
    state[...] = inbox[1]

    def last(chunk):
        @pl.when(circ < n_circ - 1)
        def _():
            hop(1, 1, chunk).start()

    sweep(last)

    table = jnp.concatenate([solved[k] for k in range(segment)], axis=1)
    upper, lower, power = code(table)
    whole, low, high = [
        jnp.concatenate([u, v], axis=0).astype(jnp.bfloat16)
        for u, v in zip(placed(upper, jnp.zeros_like(power)), placed(lower, power))
    ]

    def both(picked):
        return (256.0 * picked[:, :128] + picked[:, 128:]).astype(jnp.int32).astype(jnp.int16)

    first = both(nt(pick_recv[0], whole) + nt(pick_recv[2], low))
    second = both(nt(pick_recv[1], whole) + nt(pick_recv[2], high))
    back_sent[:, :third, :] = first.reshape(peers, third, 128)
    back_sent[:, third:, :] = second.reshape(peers, third, 128)
    start, land, drain_back = exchange(back_sent, back_arrived, back_send, back_recv)
    start()
    back_arrived[me] = back_sent[me]
    land()

    def opened(block):
        return jnp.transpose(block.reshape(peers * third, 128).astype(jnp.int32).astype(jnp.float32))

    first, second = opened(back_arrived[:, :third, :]), opened(back_arrived[:, third:, :])
    parts, _ = collect(first, second, pick_send)
    tail = width + half
    marks = (first[tail : tail + 8], second[tail : tail + 8], first[tail : tail + 8])
    total = sum(nn(decode(parts[t], marks[t], t // 2), pick_send[t]) for t in range(3))
    power = total[2 * width : 2 * width + 1] + total[2 * width + 1 : 2 * width + 2]
    root = jnp.exp2(0.5 * power)
    out_ref[...] = (256.0 * total[:width] + total[width : 2 * width]) * (1.0 / 32000.0) * root * root

    @pl.when(circ < n_circ - 1)
    def _():
        for chunk in range(2):
            hop(1, 1, chunk).wait_send()

    drain_go()
    drain_back()


def fused(elem_rows, coupling, inverses, send_rows, recv_cells, slot_counts):
    segment, width, _, lines = coupling.shape
    peers, slots = send_rows.shape[1], send_rows.shape[2]
    n_circ, n_span = lax.axis_size("circ"), lax.axis_size("span")
    third = slots // 3
    vmem = pl.BlockSpec(memory_space=pltpu.VMEM)
    hbm = pl.BlockSpec(memory_space=pl.ANY)
    boxes = pltpu.VMEM((2, width, lines), jnp.float32)
    states = pltpu.VMEM((segment, width, lines), jnp.float32)
    pick = pltpu.VMEM((3, peers * third, segment * lines), jnp.bfloat16)
    go = pltpu.VMEM((peers, 2 * third, 128), jnp.bfloat16)
    back = pltpu.VMEM((peers, 2 * third, 128), jnp.int16)
    dma = pltpu.SemaphoreType.DMA
    return pl.pallas_call(
        functools.partial(fused_kernel, n_circ, n_span),
        out_shape=jax.ShapeDtypeStruct(elem_rows.shape, jnp.float32),
        in_specs=[vmem, vmem, vmem, vmem, hbm, hbm],
        out_specs=vmem,
        scratch_shapes=[
            pltpu.VMEM(inverses.shape, jnp.bfloat16),
            pltpu.VMEM(coupling.shape, jnp.bfloat16),
            pltpu.VMEM(coupling.shape, jnp.bfloat16),
            pltpu.VMEM((16 * (width + 8), lines), jnp.float32),
            pltpu.VMEM((2, width, lines), jnp.float32),
            pltpu.VMEM((2, width, 16, lines), jnp.bfloat16),
            pltpu.VMEM((segment, width, lines), jnp.bfloat16),
            states,
            states,
            pltpu.VMEM((width, lines), jnp.float32),
            boxes,
            pick,
            pick,
            go,
            go,
            back,
            back,
            dma((segment,)),
            dma((segment,)),
            dma((2, 2)),
            dma((2, 2)),
            dma((peers,)),
            dma((peers,)),
            dma((peers,)),
            dma((peers,)),
        ],
        compiler_params=pltpu.CompilerParams(
            collective_id=1, has_side_effects=True, vmem_limit_bytes=60 * 1024 * 1024
        ),
        name="smooth",
    )(elem_rows, send_rows[0], recv_cells[0], slot_counts, inverses, coupling)


def packs(width, slots, cells, lines):
    return slots % 48 == 0 and width % 16 == 0 and width + width // 2 + 8 == 128 and lines == 128


def local(*arrays):
    coupling, send_rows = arrays[1], arrays[3]
    if packs(coupling.shape[1], send_rows.shape[2], arrays[0].shape[1], coupling.shape[3]):
        return fused(*arrays)
    return staged(*arrays)


def solution(mesh):
    return jax.shard_map(
        local,
        mesh=mesh,
        in_specs=(
            P(None, ("circ", "span")),
            P("circ", None, None, "span"),
            P("circ", None, None, "span"),
            P(("circ", "span"), None, None),
            P(("circ", "span"), None, None),
            P(("circ", "span"), None),
        ),
        out_specs=P(None, ("circ", "span")),
        check_vma=False,
    )
```

```python
import functools

import jax
import jax.numpy as jnp
from jax import lax
from jax.experimental import pallas as pl
from jax.experimental.pallas import tpu as pltpu
from jax.sharding import PartitionSpec as P

MESH = pl.DeviceIdType.MESH


def merge(low, high, half, mask):
    if 2 * half == low.shape[0]:
        return jnp.where(mask, low, high) + pltpu.roll(jnp.where(mask, high, low), half, axis=0)
    back = low.shape[0] - half
    return jnp.where(mask, low + pltpu.roll(low, back, axis=0), high + pltpu.roll(high, half, axis=0))


def fold(parts):
    row = lax.broadcasted_iota(jnp.int32, parts[0].shape, 0)
    half = len(parts) // 2
    while half:
        mask = (row & half) == 0
        parts = [merge(parts[i], parts[i + half], half, mask) for i in range(half)]
        half //= 2
    return parts[0]


def block_rows(mat_ref, position, base, vector):
    width = vector.shape[0]
    parts = []
    for i in range(8):
        total = None
        for start in range(0, width, 16):
            piece = mat_ref[position, base + i, start : start + 16, :]
            term = piece.astype(jnp.float32) * vector[start : start + 16]
            total = term if total is None else total + term
        parts.append(total[:8] + total[8:])
    return fold(parts)


def relay_kernel(
    n_circ, rows_ref, inv_hbm, coup_hbm, out_ref, inv, coup, forcing, state, inbox, outbox, inv_sem, coup_sem, send_sem, recv_sem
):
    me = lax.axis_index("circ")
    right, left = lax.rem(me + 1, n_circ), lax.rem(me + n_circ - 1, n_circ)
    segment, width = coup.shape[0], coup.shape[1]
    blocks = width // 8

    loads = [pltpu.make_async_copy(inv_hbm.at[k], inv.at[k], inv_sem.at[k]) for k in range(segment)]
    loads += [pltpu.make_async_copy(coup_hbm.at[k], coup.at[k], coup_sem.at[k]) for k in range(segment)]
    for load in loads:
        load.start()

    barrier = pltpu.get_barrier_semaphore()
    for neighbour in (left, right):
        pl.semaphore_signal(barrier, inc=1, device_id={"circ": neighbour}, device_id_type=MESH)
    pl.semaphore_wait(barrier, 2)

    for k in range(segment):
        loads[k].wait()
        vector = rows_ref[k].astype(jnp.float32)

        def force(b, _, k=k, vector=vector):
            base = pl.multiple_of(b * 8, 8)
            forcing[k, pl.ds(base, 8), :] = block_rows(inv, k, base, vector)
            return 0

        lax.fori_loop(0, blocks, force, 0)
    for k in range(segment):
        loads[segment + k].wait()

    def hop(turn, slot):
        return pltpu.make_async_remote_copy(
            src_ref=outbox.at[turn],
            dst_ref=inbox.at[slot],
            send_sem=send_sem.at[turn],
            recv_sem=recv_sem.at[slot],
            device_id={"circ": right},
            device_id_type=MESH,
        )

    def sweep(target):
        def step(k, _):
            vector = state[...]

            def advance(b, _):
                base = pl.multiple_of(b * 8, 8)
                value = forcing[k, pl.ds(base, 8), :] + block_rows(coup, k, base, vector)
                state[pl.ds(base, 8), :] = value
                if target is not None:
                    target[k, pl.ds(base, 8), :] = value
                return 0

            lax.fori_loop(0, blocks, advance, 0)
            return 0

        lax.fori_loop(0, segment, step, 0)

    @pl.when(me == 0)
    def _():
        state[...] = jnp.zeros_like(state)

    @pl.when(me > 0)
    def _():
        hop(0, 0).wait_recv()
        state[...] = inbox[0]

    sweep(None)
    outbox[0] = state[...]
    slot = jnp.where(me == n_circ - 1, 1, 0)
    first = hop(0, slot)
    first.start()
    hop(0, 1).wait_recv()
    state[...] = inbox[1]
    sweep(out_ref)

    @pl.when(me < n_circ - 1)
    def _():
        outbox[1] = state[...]
        second = hop(1, 1)
        second.start()
        second.wait_send()

    first.wait_send()


def relay(rows, inverses, coupling):
    segment, width, _, lines = coupling.shape
    n_circ = lax.axis_size("circ")
    state = pltpu.VMEM((width, lines), jnp.float32)
    boxes = pltpu.VMEM((2, width, lines), jnp.float32)
    return pl.pallas_call(
        functools.partial(relay_kernel, n_circ),
        out_shape=jax.ShapeDtypeStruct((segment, width, lines), jnp.float32),
        in_specs=[
            pl.BlockSpec(memory_space=pltpu.VMEM),
            pl.BlockSpec(memory_space=pl.ANY),
            pl.BlockSpec(memory_space=pl.ANY),
        ],
        out_specs=pl.BlockSpec(memory_space=pltpu.VMEM),
        scratch_shapes=[
            pltpu.VMEM(inverses.shape, jnp.bfloat16),
            pltpu.VMEM(coupling.shape, jnp.bfloat16),
            pltpu.VMEM((segment, width, lines), jnp.float32),
            state,
            boxes,
            boxes,
            pltpu.SemaphoreType.DMA((segment,)),
            pltpu.SemaphoreType.DMA((segment,)),
            pltpu.SemaphoreType.DMA((2,)),
            pltpu.SemaphoreType.DMA((2,)),
        ],
        compiler_params=pltpu.CompilerParams(
            collective_id=0, has_side_effects=True, vmem_limit_bytes=48 * 1024 * 1024
        ),
        name="relay",
    )(rows, inverses, coupling)


def staged(elem_rows, coupling, inverses, send_rows, recv_cells, slot_counts):
    features, cell_count = elem_rows.shape
    peer_count, slot_count = (send_rows.shape[1], send_rows.shape[2])
    segment, line_count = (coupling.shape[0], coupling.shape[3])
    outgoing = jnp.take(elem_rows, send_rows[0].reshape(-1), axis=1).reshape(
        features, peer_count, slot_count
    )
    arrived = lax.all_to_all(outgoing, ("circ", "span"), split_axis=1, concat_axis=1, tiled=True)
    filled = jnp.arange(slot_count, dtype=jnp.int32)[None, :] < slot_counts[0][:, None]
    targets = jnp.where(filled, recv_cells[0], cell_count).reshape(-1)
    line_rows = (
        jnp.zeros((features, cell_count), jnp.bfloat16)
        .at[:, targets]
        .set(arrived.reshape(features, -1), mode="drop")
    )
    line_cells = jnp.transpose(line_rows.reshape(features, segment, line_count), (1, 0, 2))
    states = relay(line_cells, inverses, coupling)
    solved = jnp.transpose(states, (1, 0, 2)).reshape(features, cell_count)
    returning = jnp.take(solved, recv_cells[0].reshape(-1), axis=1).reshape(
        features, peer_count, slot_count
    )
    returning = jnp.where(filled[None, :, :], returning, 0.0)
    returned = lax.all_to_all(returning, ("circ", "span"), split_axis=1, concat_axis=1, tiled=True)
    return (
        jnp.zeros((features, cell_count), jnp.float32)
        .at[:, send_rows[0].reshape(-1)]
        .add(returned.reshape(features, -1))
    )


def code(table):
    top = jnp.max(jnp.abs(table), axis=0, keepdims=True)
    power = jnp.ceil(jnp.log2(jnp.maximum(top, jnp.float32(1e-36))))
    root = jnp.exp2(-0.5 * power)
    whole = jnp.round(table * root * root * 32000.0)
    upper = jnp.round(whole * (1.0 / 256.0))
    return upper, whole - 256.0 * upper, power


def placed(table, power):
    parts = spread(table)
    width, cells = table.shape
    start = width + width // 2
    row = lax.broadcasted_iota(jnp.int32, (8, cells), 0)
    marks = [jnp.where(row == spot, power, 0.0) for spot in (0, 1, 1)]
    return [jnp.concatenate([part[:start], mark], axis=0) for part, mark in zip(parts, marks)]


def decode(whole, marks, spot):
    upper = jnp.round(whole * (1.0 / 256.0))
    row = lax.broadcasted_iota(jnp.int32, marks.shape, 0)
    power = jnp.where(row == spot, marks, 0.0)
    return jnp.concatenate([upper, whole - 256.0 * upper, power, jnp.zeros_like(power)], axis=0).astype(jnp.bfloat16)


def split(values):
    high = values.astype(jnp.bfloat16)
    return high, (values - high.astype(jnp.float32)).astype(jnp.bfloat16)


def nt(a, b):
    return lax.dot_general(a, b, (((1,), (1,)), ((), ())), preferred_element_type=jnp.float32)


def nn(a, b):
    return jnp.dot(a, b, preferred_element_type=jnp.float32)


def spread(table):
    width, cells = table.shape
    half = width // 2
    head = jnp.zeros((width, cells), jnp.float32)
    tail = jnp.zeros((128 - width - half, cells), jnp.float32)
    return (
        jnp.concatenate([table, jnp.zeros((128 - width, cells), jnp.float32)], axis=0),
        jnp.concatenate([head, table[:half], tail], axis=0),
        jnp.concatenate([head, table[half:], tail], axis=0),
    )


def flip_block(source, target, flat, position, block):
    width = source.shape[2]
    for i in range(16):
        for start in range(0, width, 16):
            piece = source[position, block * 16 + i, start : start + 16, :].astype(jnp.float32)
            flat[(width + 8) * i + start : (width + 8) * i + start + 16, :] = piece
    rows = pl.ds(pl.multiple_of(block * 16, 16), 16)
    for j in range(width):
        target[position, j, rows, :] = flat[pl.ds(j, 16, stride=width + 8), :].astype(jnp.bfloat16)


def columns(matrix, position, planes, spots):
    width, count = planes.shape[1], planes.shape[0]

    def run(tile, first, last):
        total = None
        for j in range(first, last):
            for p in range(count):
                spot = spots[p, j].astype(jnp.float32)
                term = matrix[position, j, 16 * tile : 16 * tile + 16, :].astype(jnp.float32) * spot
                total = term if total is None else total + term
        return total

    for j in range(width):
        for p in range(count):
            spots[p, j] = jnp.broadcast_to(planes[p, j : j + 1, :], (16, planes.shape[2])).astype(jnp.bfloat16)
    tiles = width // 16
    whole = tiles // 4 * 4
    totals = [run(tile, 0, width) for tile in range(whole)]
    for tile in range(whole, tiles):
        cuts = [width * q // 4 for q in range(5)]
        quarters = [run(tile, cuts[q], cuts[q + 1]) for q in range(4)]
        totals.append((quarters[0] + quarters[1]) + (quarters[2] + quarters[3]))
    return jnp.concatenate(totals, axis=0)


def fused_kernel(
    n_circ, n_span, elem_ref, send_ref, recv_ref, count_ref, inv_hbm, coup_hbm, out_ref,
    inv, coup, wide, flat, planes, spots, line_rows, forcing, solved, state, inbox, pick_send, pick_recv, sent, arrived, back_sent, back_arrived,
    inv_sem, coup_sem, send_sem, recv_sem, go_send, go_recv, back_send, back_recv,
):
    circ, span = lax.axis_index("circ"), lax.axis_index("span")
    peers = n_circ * n_span
    me = circ * n_span + span
    right = lax.rem(circ + 1, n_circ)
    segment, width, lines = forcing.shape
    cells = segment * lines
    third = sent.shape[1] // 2
    half = width // 2
    blocks = width // 8

    coup_loads = [pltpu.make_async_copy(coup_hbm.at[k], coup.at[k], coup_sem.at[k]) for k in range(segment)]
    inv_loads = [pltpu.make_async_copy(inv_hbm.at[k], inv.at[k], inv_sem.at[k]) for k in range(segment)]
    barrier = pltpu.get_barrier_semaphore()

    def greet(o, _):
        peer = lax.rem(me + o, peers)
        pl.semaphore_signal(
            barrier, inc=1, device_id={"circ": peer // n_span, "span": peer % n_span}, device_id_type=MESH
        )
        return 0

    lax.fori_loop(1, peers, greet, 0)

    for load in coup_loads + inv_loads:
        load.start()

    def build(index_ref, pick, masked):
        lane = lax.broadcasted_iota(jnp.int32, (third, index_ref.shape[1]), 1)
        slot = lax.broadcasted_iota(jnp.int32, (third, index_ref.shape[1]), 0)
        number = lax.broadcasted_iota(jnp.int32, (third, cells), 1).astype(jnp.float32)
        owner = lax.broadcasted_iota(jnp.int32, count_ref.shape, 1)
        rank = lax.broadcasted_iota(jnp.int32, (third, 1), 0).astype(jnp.float32)

        def one(p, _):
            row = index_ref[pl.ds(p, 1), :].astype(jnp.float32)
            if masked:
                counts = count_ref[...].astype(jnp.float32)
                count = jnp.sum(jnp.where(owner == p, counts, 0.0), axis=1, keepdims=True)
            for t in range(3):
                column = jnp.sum(jnp.where(lane == slot + t * third, row, 0.0), axis=1, keepdims=True)
                if masked:
                    column = jnp.where(rank + float(t * third) < count, column, -1.0)
                hot = jnp.where(number == column, 1.0, 0.0).astype(jnp.bfloat16)
                pick[t, pl.ds(pl.multiple_of(p * third, third), third), :] = hot
            return 0

        lax.fori_loop(0, peers, one, 0)

    def exchange(outs, ins, outs_sem, ins_sem):
        def copy(peer, landing):
            return pltpu.make_async_remote_copy(
                src_ref=outs.at[peer],
                dst_ref=ins.at[landing],
                send_sem=outs_sem.at[peer],
                recv_sem=ins_sem.at[landing],
                device_id={"circ": peer // n_span, "span": peer % n_span},
                device_id_type=MESH,
            )

        def start(o, _):
            copy(lax.rem(me + o, peers), me).start()
            return 0

        def land(o, _):
            peer = lax.rem(me + peers - o, peers)
            copy(peer, peer).wait_recv()
            return 0

        def drain(o, _):
            copy(lax.rem(me + o, peers), me).wait_send()
            return 0

        return (
            lambda: lax.fori_loop(1, peers, start, 0),
            lambda: lax.fori_loop(1, peers, land, 0),
            lambda: lax.fori_loop(1, peers, drain, 0),
        )

    build(send_ref, pick_send, False)
    whole, low, high = [w.astype(jnp.bfloat16) for w in spread(elem_ref[...].astype(jnp.float32))]
    first = nt(pick_send[0], whole) + nt(pick_send[2], low)
    second = nt(pick_send[1], whole) + nt(pick_send[2], high)
    sent[:, :third, :] = first.astype(jnp.bfloat16).reshape(peers, third, 128)
    sent[:, third:, :] = second.astype(jnp.bfloat16).reshape(peers, third, 128)

    pl.semaphore_wait(barrier, peers - 1)
    start, land, drain_go = exchange(sent, arrived, go_send, go_recv)
    start()
    arrived[me] = sent[me]
    build(recv_ref, pick_recv, True)
    for k in range(segment):
        coup_loads[k].wait()

        def widen(b, _, k=k):
            flip_block(coup, wide, flat, k, b)
            return 0

        lax.fori_loop(0, width // 16, widen, 0)
    land()

    def turned(block):
        return jnp.transpose(block.reshape(peers * third, 128).astype(jnp.float32))

    first, second = turned(arrived[:, :third, :]), turned(arrived[:, third:, :])

    def collect(first, second, pick):
        extra = jnp.concatenate([first[width : width + half], second[width : width + half]], axis=0)
        parts = [first[:width], second[:width], extra]
        return parts, pick

    parts, _ = collect(first, second, pick_recv)
    line = sum(nn(parts[t].astype(jnp.bfloat16), pick_recv[t]) for t in range(3))

    for k in range(segment):
        line_rows[k] = line[:, k * lines : (k + 1) * lines].astype(jnp.bfloat16)
    for k in range(segment):
        inv_loads[k].wait()
        vector = line_rows[k].astype(jnp.float32)

        def force(b, _, k=k, vector=vector):
            for base in (pl.multiple_of(b * 16, 16), pl.multiple_of(b * 16 + 8, 8)):
                forcing[k, pl.ds(base, 8), :] = block_rows(inv, k, base, vector)
            return 0

        lax.fori_loop(0, blocks // 2, force, 0)

    cut = (blocks // 4) * 16
    chunks = ((0, cut), (cut, width))

    def hop(turn, slot, chunk):
        rows = pl.ds(chunks[chunk][0], chunks[chunk][1] - chunks[chunk][0])
        return pltpu.make_async_remote_copy(
            src_ref=solved.at[segment - 1, rows],
            dst_ref=inbox.at[slot, rows],
            send_sem=send_sem.at[turn, chunk],
            recv_sem=recv_sem.at[slot, chunk],
            device_id={"circ": right},
            device_id_type=MESH,
        )

    def sweep(emit):
        value = state[...]
        for k in range(segment):
            high, low = split(value)
            planes[0] = high.astype(jnp.float32)
            planes[1] = low.astype(jnp.float32)
            value = forcing[k] + columns(wide, k, planes, spots)
            solved[k] = value
        for chunk in range(2):
            emit(chunk)

    @pl.when(circ == 0)
    def _():
        state[...] = jnp.zeros_like(state)

    @pl.when(circ > 0)
    def _():
        for chunk in range(2):
            hop(0, 0, chunk).wait_recv()
        state[...] = inbox[0]

    landing = jnp.where(circ == n_circ - 1, 1, 0)
    sweep(lambda chunk: hop(0, landing, chunk).start())
    for chunk in range(2):
        hop(0, 1, chunk).wait_send()
    for chunk in range(2):
        hop(0, 1, chunk).wait_recv()
    state[...] = inbox[1]

    def last(chunk):
        @pl.when(circ < n_circ - 1)
        def _():
            hop(1, 1, chunk).start()

    sweep(last)

    table = jnp.concatenate([solved[k] for k in range(segment)], axis=1)
    upper, lower, power = code(table)
    whole, low, high = [
        jnp.concatenate([u, v], axis=0).astype(jnp.bfloat16)
        for u, v in zip(placed(upper, jnp.zeros_like(power)), placed(lower, power))
    ]

    def both(picked):
        return (256.0 * picked[:, :128] + picked[:, 128:]).astype(jnp.int32).astype(jnp.int16)

    first = both(nt(pick_recv[0], whole) + nt(pick_recv[2], low))
    second = both(nt(pick_recv[1], whole) + nt(pick_recv[2], high))
    back_sent[:, :third, :] = first.reshape(peers, third, 128)
    back_sent[:, third:, :] = second.reshape(peers, third, 128)
    start, land, drain_back = exchange(back_sent, back_arrived, back_send, back_recv)
    start()
    back_arrived[me] = back_sent[me]
    land()

    def opened(block):
        return jnp.transpose(block.reshape(peers * third, 128).astype(jnp.int32).astype(jnp.float32))

    first, second = opened(back_arrived[:, :third, :]), opened(back_arrived[:, third:, :])
    parts, _ = collect(first, second, pick_send)
    tail = width + half
    marks = (first[tail : tail + 8], second[tail : tail + 8], first[tail : tail + 8])
    total = sum(nn(decode(parts[t], marks[t], t // 2), pick_send[t]) for t in range(3))
    power = total[2 * width : 2 * width + 1] + total[2 * width + 1 : 2 * width + 2]
    root = jnp.exp2(0.5 * power)
    out_ref[...] = (256.0 * total[:width] + total[width : 2 * width]) * (1.0 / 32000.0) * root * root

    @pl.when(circ < n_circ - 1)
    def _():
        for chunk in range(2):
            hop(1, 1, chunk).wait_send()

    drain_go()
    drain_back()


def fused(elem_rows, coupling, inverses, send_rows, recv_cells, slot_counts):
    segment, width, _, lines = coupling.shape
    peers, slots = send_rows.shape[1], send_rows.shape[2]
    n_circ, n_span = lax.axis_size("circ"), lax.axis_size("span")
    third = slots // 3
    vmem = pl.BlockSpec(memory_space=pltpu.VMEM)
    hbm = pl.BlockSpec(memory_space=pl.ANY)
    boxes = pltpu.VMEM((2, width, lines), jnp.float32)
    states = pltpu.VMEM((segment, width, lines), jnp.float32)
    pick = pltpu.VMEM((3, peers * third, segment * lines), jnp.bfloat16)
    go = pltpu.VMEM((peers, 2 * third, 128), jnp.bfloat16)
    back = pltpu.VMEM((peers, 2 * third, 128), jnp.int16)
    dma = pltpu.SemaphoreType.DMA
    return pl.pallas_call(
        functools.partial(fused_kernel, n_circ, n_span),
        out_shape=jax.ShapeDtypeStruct(elem_rows.shape, jnp.float32),
        in_specs=[vmem, vmem, vmem, vmem, hbm, hbm],
        out_specs=vmem,
        scratch_shapes=[
            pltpu.VMEM(inverses.shape, jnp.bfloat16),
            pltpu.VMEM(coupling.shape, jnp.bfloat16),
            pltpu.VMEM(coupling.shape, jnp.bfloat16),
            pltpu.VMEM((16 * (width + 8), lines), jnp.float32),
            pltpu.VMEM((2, width, lines), jnp.float32),
            pltpu.VMEM((2, width, 16, lines), jnp.bfloat16),
            pltpu.VMEM((segment, width, lines), jnp.bfloat16),
            states,
            states,
            pltpu.VMEM((width, lines), jnp.float32),
            boxes,
            pick,
            pick,
            go,
            go,
            back,
            back,
            dma((segment,)),
            dma((segment,)),
            dma((2, 2)),
            dma((2, 2)),
            dma((peers,)),
            dma((peers,)),
            dma((peers,)),
            dma((peers,)),
        ],
        compiler_params=pltpu.CompilerParams(
            collective_id=1, has_side_effects=True, vmem_limit_bytes=60 * 1024 * 1024
        ),
        name="smooth",
    )(elem_rows, send_rows[0], recv_cells[0], slot_counts, inverses, coupling)


def packs(width, slots, cells, lines):
    return slots % 48 == 0 and width % 16 == 0 and width + width // 2 + 8 == 128 and lines == 128


def local(*arrays):
    coupling, send_rows = arrays[1], arrays[3]
    if packs(coupling.shape[1], send_rows.shape[2], arrays[0].shape[1], coupling.shape[3]):
        return fused(*arrays)
    return staged(*arrays)


def solution(mesh):
    return jax.shard_map(
        local,
        mesh=mesh,
        in_specs=(
            P(None, ("circ", "span")),
            P("circ", None, None, "span"),
            P("circ", None, None, "span"),
            P(("circ", "span"), None, None),
            P(("circ", "span"), None, None),
            P(("circ", "span"), None),
        ),
        out_specs=P(None, ("circ", "span")),
        check_vma=False,
    )
```
